768 devices in a mesh: dp: 128 (over z_hi, x, y), space: 6 (over z_lo, core).
Axes of the slice: x: 4, y: 8, z: 12 (z_hi: 4, z_lo: 3; z = z_hi * 3 + z_lo), core: 2. Of those that a mesh axis runs over, the one named last changes fastest.
Arguments:
- fields: bfloat16 [128, 126, 252, 192], P('dp', 'space'), may hold values from -6 to 6
- cotangent: bfloat16 [128, 126, 252, 192], P('dp', 'space'), may hold values from -1.796875 to 1.796875
- spec_real: bfloat16 [126, 192], replicated, may hold values from -4.1875 to 4.1875
- spec_imag: bfloat16 [126, 192], replicated, may hold values from -4.1875 to 4.1875
Outputs:
- grad_real: float32 [126, 192], replicated
- grad_imag: float32 [126, 192], replicated
The draws below stay inside these ranges and needn't reach their ends.
All inputs are finite; a program needn't handle non-finite values.
Results may differ from the reference program's by a relative error of at most 0.015.
Values may be sent and summed in bfloat16 or wider, within the bound.
A program may use at most 64 MiB of HBM per device.

```python
import math
import jax
import jax.numpy as jnp
from jax import lax

C = 192
NLAT = 126
NLON = 252
MODES = 126
BATCH = 128


def block_levels(rng, shape, cuts, least, largest):
    gain = 1.0
    for position, parts in cuts:
        draws = jax.random.uniform(jax.random.fold_in(jax.random.fold_in(rng, 6), position), (parts,), jnp.float32, least / len(cuts), largest / len(cuts))
        gain = gain * jnp.repeat(jnp.exp(draws), shape[position] // parts).reshape((-1,) + (1,) * (len(shape) - 1 - position))
    return gain


def gaussian(stream_key, extent, spread, most, pieces=(), kind=jnp.bfloat16):
    array = spread * jax.random.normal(stream_key, extent, jnp.float32)
    if pieces:
        array = array * block_levels(stream_key, extent, pieces, -0.22, 0.18)
    return jnp.clip(array, -most, most).astype(kind)


def setup_inputs(seed: int = 0) -> dict:
    key_list = jax.random.split(jax.random.key(seed), 5)
    fields = gaussian(key_list[0], (BATCH, NLAT, NLON, C), 1.0, 6.0, ((0, 128), (1, 6)))
    cotangent = gaussian(key_list[1], (BATCH, NLAT, NLON, C), 0.3, 1.796875, ((0, 128), (1, 6)))
    spec_real = gaussian(key_list[2], (MODES, C), 0.7, 4.1875)
    spec_imag = gaussian(key_list[3], (MODES, C), 0.7, 4.1875)
    return {"fields": fields, "cotangent": cotangent, "spec_real": spec_real, "spec_imag": spec_imag}


def grid_tables():
    latitude = jnp.arange(NLAT, dtype=jnp.float32)
    colatitude = math.pi * (latitude + 0.5) / NLAT
    sin_theta = jnp.sin(colatitude)
    quad_weight = math.pi / NLAT * (2.0 * math.pi / NLON) * sin_theta
    return (jnp.cos(colatitude), sin_theta, quad_weight)

def fourier_tables(orders):
    longitude = jnp.arange(NLON, dtype=jnp.int32)
    phase_index = orders[:, None] * longitude[None, :] % NLON
    angles = 2.0 * math.pi / NLON * phase_index.astype(jnp.float32)
    basis_rows = jnp.stack([jnp.cos(angles), -jnp.sin(angles)], axis=1)
    factor = jnp.where(orders == 0, 1.0, 2.0).astype(jnp.float32)
    return (basis_rows.astype(jnp.bfloat16), (basis_rows * factor[:, None, None]).astype(jnp.bfloat16))

def legendre(orders, cos_theta, sin_theta):
    counters = jnp.arange(1, MODES, dtype=jnp.float32)
    log_steps = 0.5 * jnp.log((2.0 * counters + 1.0) / (2.0 * counters))
    log_table = jnp.concatenate([jnp.zeros((1,), jnp.float32), jnp.cumsum(log_steps)])
    order_float = orders.astype(jnp.float32)[:, None]
    log_diagonal = 0.5 * jnp.log(1.0 / (4.0 * math.pi)) + log_table[orders][:, None] + order_float * jnp.log(sin_theta)[None, :]
    diagonal_start = jnp.exp(log_diagonal)
    cos_row = cos_theta[None, :]

    def advance(state_pair, degree):
        previous, earlier = state_pair
        degree_float = degree.astype(jnp.float32)
        growth = jnp.sqrt(jnp.maximum(4.0 * degree_float * degree_float - 1.0, 0.0) / jnp.maximum(degree_float * degree_float - order_float * order_float, 1.0))
        below = degree_float - 1.0
        damping = jnp.sqrt(jnp.maximum(below * below - order_float * order_float, 0.0) / jnp.maximum(4.0 * below * below - 1.0, 1.0))
        recurrence = growth * (cos_row * previous - damping * earlier)
        current = jnp.where(degree_float == order_float, diagonal_start, jnp.where(degree_float > order_float, recurrence, 0.0))
        return ((current, previous), current)
    empty_rows = jnp.zeros_like(diagonal_start)
    final_state, stacked = lax.scan(advance, (empty_rows, empty_rows), jnp.arange(MODES, dtype=jnp.int32), unroll=6)
    return jnp.swapaxes(stacked, 0, 1)

def gelu_slope(values):
    cumulative = 0.5 * (1.0 + lax.erf(values / math.sqrt(2.0)))
    density = jnp.exp(-0.5 * values * values) / math.sqrt(2.0 * math.pi)
    return cumulative + values * density

def reference(fields, cotangent, spec_real, spec_imag):
    cos_theta, sin_theta, quad_weight = grid_tables()
    orders = jnp.arange(MODES, dtype=jnp.int32)
    forward_basis, inverse_basis = fourier_tables(orders)
    associated = legendre(orders, cos_theta, sin_theta)
    weighted = (associated * quad_weight[None, None, :]).astype(jnp.bfloat16).astype(jnp.float32)
    plain = associated.astype(jnp.bfloat16).astype(jnp.float32)
    forward_wide = forward_basis.astype(jnp.float32)
    inverse_wide = inverse_basis.astype(jnp.float32)
    filter_real = spec_real.astype(jnp.float32)[None]
    filter_imag = spec_imag.astype(jnp.float32)[None]

    def one_sample(inputs_pair):
        sample, incoming = inputs_pair
        coeffs = jnp.einsum('alc,mpl->mapc', sample.astype(jnp.float32), forward_wide)
        coeffs = coeffs.reshape(MODES, NLAT, 2 * C).astype(jnp.bfloat16)
        spectral = jnp.einsum('mlj,mjc->mlc', weighted, coeffs.astype(jnp.float32)).astype(jnp.bfloat16)
        spec_values = spectral.astype(jnp.float32)
        real_part = spec_values[..., :C]
        imag_part = spec_values[..., C:]
        mixed = jnp.concatenate([real_part * filter_real - imag_part * filter_imag, real_part * filter_imag + imag_part * filter_real], axis=-1).astype(jnp.bfloat16)
        synthesized = jnp.einsum('mlj,mlc->mjc', plain, mixed.astype(jnp.float32)).astype(jnp.bfloat16)
        signal = jnp.einsum('mapc,mpl->alc', synthesized.reshape(MODES, NLAT, 2, C).astype(jnp.float32), inverse_wide)
        upstream = (incoming.astype(jnp.float32) * gelu_slope(signal)).astype(jnp.bfloat16)
        back_coeffs = jnp.einsum('alc,mpl->mapc', upstream.astype(jnp.float32), inverse_wide)
        back_coeffs = back_coeffs.reshape(MODES, NLAT, 2 * C).astype(jnp.bfloat16)
        back_spectral = jnp.einsum('mlj,mjc->mlc', plain, back_coeffs.astype(jnp.float32)).astype(jnp.bfloat16)
        back_values = back_spectral.astype(jnp.float32)
        back_real = back_values[..., :C]
        back_imag = back_values[..., C:]
        real_term = lax.optimization_barrier(jnp.sum(real_part * back_real + imag_part * back_imag, axis=0))
        imag_term = lax.optimization_barrier(jnp.sum(real_part * back_imag - imag_part * back_real, axis=0))
        return (real_term, imag_term)
    real_terms, imag_terms = lax.map(one_sample, (fields, cotangent))
    grad_real = lax.optimization_barrier(jnp.sum(real_terms, axis=0)) / BATCH
    grad_imag = lax.optimization_barrier(jnp.sum(imag_terms, axis=0)) / BATCH
    return (grad_real, grad_imag)
```

```python
import functools
import math

import jax
import jax.numpy as jnp
import ml_dtypes
import numpy as np
from jax import lax
from jax.experimental import pallas as pl
from jax.experimental.pallas import tpu as pltpu
from jax.sharding import PartitionSpec as P

NLAT = 126
NLON = 252
MODES = 126
CHANNELS = 192
HALF = 63
PARTS = 6
BAND = 21
SLICE = 32
ROWS = 64
LANES = 128
MESH = pl.DeviceIdType.MESH
NT = (((1,), (1,)), ((), ()))
NN = (((1,), (0,)), ((), ()))


def legendre_table(theta):
    counters = np.arange(1, MODES, dtype=np.float64)
    steps = 0.5 * np.log((2.0 * counters + 1.0) / (2.0 * counters))
    log_table = np.concatenate([np.zeros(1), np.cumsum(steps)])
    orders = np.arange(MODES, dtype=np.float64)[:, None]
    diagonal = np.exp(
        0.5 * np.log(1.0 / (4.0 * math.pi))
        + log_table[:, None]
        + orders * np.log(np.sin(theta))[None, :]
    )
    cosine = np.cos(theta)[None, :]
    previous = np.zeros_like(diagonal)
    earlier = np.zeros_like(diagonal)
    table = np.zeros((MODES, MODES, theta.size))
    for degree in range(MODES):
        growth = np.sqrt(
            max(4.0 * degree * degree - 1.0, 0.0)
            / np.maximum(degree * degree - orders * orders, 1.0)
        )
        below = degree - 1.0
        damping = np.sqrt(
            np.maximum(below * below - orders * orders, 0.0)
            / max(4.0 * below * below - 1.0, 1.0)
        )
        current = growth * (cosine * previous - damping * earlier)
        current = np.where(
            orders == degree, diagonal, np.where(orders < degree, current, 0.0)
        )
        table[:, degree] = current
        previous, earlier = current, previous
    return table


def tables():
    theta = math.pi * (np.arange(HALF) + 0.5) / NLAT
    weight = np.zeros(ROWS, np.float32)
    weight[:HALF] = math.pi / NLAT * (2.0 * math.pi / NLON) * np.sin(theta)
    plain = np.zeros((MODES, ROWS, LANES), np.float32)
    plain[:, :HALF, :MODES] = legendre_table(theta).transpose(0, 2, 1)
    orders = np.arange(MODES)
    phase = orders[:, None] * np.arange(NLON)[None, :] % NLON
    angles = 2.0 * math.pi / NLON * phase
    basis = np.zeros((2, LANES, NLON), np.float32)
    basis[0, :MODES] = np.cos(angles)
    basis[1, :MODES] = -np.sin(angles)
    factor = np.full((LANES, 1), 2.0, np.float32)
    factor[0] = 1.0
    forward = basis.astype(ml_dtypes.bfloat16)
    inverse = (forward.astype(np.float32) * factor).astype(ml_dtypes.bfloat16)
    return weight, plain.astype(ml_dtypes.bfloat16), forward, inverse


def gelu_slope(values):
    cumulative = 0.5 * (1.0 + lax.erf(values * (1.0 / math.sqrt(2.0))))
    density = jnp.exp(-0.5 * values * values) * (1.0 / math.sqrt(2.0 * math.pi))
    return cumulative + values * density


def dot(a, b, dims=NN):
    return lax.dot_general(a, b, dims, preferred_element_type=jnp.float32)


def kernel(
    grid_dims,
    scale,
    weight_ref,
    fields_ref,
    cot_ref,
    plain_hbm,
    forward_ref,
    inverse_ref,
    real_ref,
    imag_ref,
    out_real,
    out_imag,
    field,
    cot,
    plain,
    turned,
    work,
    slope,
    spec,
    swap,
    filt,
    acc,
    packed,
    xbuf,
    ybuf,
    zbuf,
    mine,
    gathered,
    local_sem,
    send_f,
    recv_f,
    send_c,
    recv_c,
    send_x,
    recv_x,
    send_y,
    recv_y,
    send_z,
    recv_z,
    send_s,
    recv_s,
    send_g,
    recv_g,
):
    n_z, n_x, n_y = grid_dims
    rows = ROWS // n_x
    me = lax.axis_index("space")
    dp = lax.axis_index("dp")
    zi = dp // (n_x * n_y)
    xi = lax.rem(dp // n_y, n_x)
    yi = lax.rem(dp, n_y)
    chip, core = me // 2, lax.rem(me, 2)
    first = jnp.where(chip == 0, 2, 0)
    second = 3 - chip - first
    space_peers = [
        2 * first + core,
        2 * first + 1 - core,
        2 * second + core,
        2 * second + 1 - core,
        2 * chip + 1 - core,
    ]
    x_peers = [lax.rem(xi + r, n_x) for r in range(1, n_x)]
    y_peers = [lax.rem(yi + r, n_y) for r in range(1, n_y)]
    z_peers = [lax.rem(zi + r, n_z) for r in range(1, n_z)]

    def at_x(x):
        return {"dp": (zi * n_x + x) * n_y + yi}

    def at_y(y):
        return {"dp": (zi * n_x + xi) * n_y + y}

    def at_z(z):
        return {"dp": (z * n_x + xi) * n_y + yi}

    everyone = (
        [{"space": s} for s in space_peers]
        + [at_x(x) for x in x_peers]
        + [at_y(y) for y in y_peers]
        + [at_z(z) for z in z_peers]
    )
    barrier = pltpu.get_barrier_semaphore()
    for target in everyone:
        pl.semaphore_signal(barrier, inc=1, device_id=target, device_id_type=MESH)

    load = pltpu.make_async_copy(plain_hbm, plain, local_sem.at[0])
    load.start()
    mine_lanes = pl.ds(pl.multiple_of(me * SLICE, SLICE), SLICE)
    own_f = pltpu.make_async_copy(
        fields_ref.at[:, mine_lanes, :], field.at[pl.ds(me * BAND, BAND)], recv_f.at[me]
    )
    own_c = pltpu.make_async_copy(
        cot_ref.at[:, mine_lanes, :], cot.at[pl.ds(me * BAND, BAND)], recv_c.at[me]
    )
    own_f.start()
    own_c.start()
    pl.semaphore_wait(barrier, len(everyone))

    def exchange(source, target, send, recv):
        copies = []
        for slot, peer in enumerate(space_peers):
            lanes = pl.ds(pl.multiple_of(peer * SLICE, SLICE), SLICE)
            copies.append(
                pltpu.make_async_remote_copy(
                    src_ref=source.at[:, lanes, :],
                    dst_ref=target.at[pl.ds(me * BAND, BAND)],
                    send_sem=send.at[slot],
                    recv_sem=recv.at[me],
                    device_id={"space": peer},
                    device_id_type=MESH,
                )
            )
            copies[-1].start()
        return copies

    sends = exchange(fields_ref, field, send_f, recv_f)
    sends += exchange(cot_ref, cot, send_c, recv_c)

    def arrive(target, recv, band):
        block = target.at[pl.ds(band * BAND, BAND)]
        pltpu.make_async_copy(block, block, recv.at[band]).wait()

    for index, source in enumerate((real_ref, imag_ref)):
        filt[index] = jnp.zeros((LANES, LANES), jnp.float32)
        values = source[mine_lanes, :].astype(jnp.float32)
        filt[index, :, :MODES] = jnp.concatenate([values] * 4, axis=0)
        filt[index] = filt[index].T
    work[pl.ds(HALF, LANES, stride=ROWS), :] = jnp.zeros((LANES, LANES), jnp.float32)
    load.wait()

    @pl.loop(0, MODES)
    def _(m):
        turned[m] = plain[m].astype(jnp.float32).T.astype(jnp.bfloat16)

    zero = jnp.zeros((SLICE, NLON), jnp.bfloat16)

    def to_modes(north, south, basis_ref, j, factor):
        cosine = jnp.concatenate([north, zero, south, zero], axis=0)
        sine = jnp.concatenate([zero, north, zero, south], axis=0)
        modes = dot(basis_ref[0], cosine, NT) + dot(basis_ref[1], sine, NT)
        if factor is not None:
            modes = modes * factor
        work[pl.ds(j, LANES, stride=ROWS), :] = modes

    for band in (2, 1, 0):
        arrive(field, recv_f, band)
        arrive(field, recv_f, PARTS - 1 - band)

        @pl.loop(0, BAND)
        def _(t, band=band):
            j = band * BAND + t
            to_modes(
                field[j], field[NLAT - 1 - j], forward_ref, j, weight_ref[j]
            )

    lane = lax.broadcasted_iota(jnp.int32, (8, LANES), 1)
    odd_group = (lax.rem(lane // SLICE, 2) == 1)[None]
    degree = lax.broadcasted_iota(jnp.int32, (8, LANES), 0)
    sign = (1 - 2 * lax.rem(degree, 2)).astype(jnp.float32)[None]

    for group in range(8):
        low = 16 * group
        depth = LANES - low
        pairs = (min(16, MODES - low)) // 2

        @pl.loop(0, pairs)
        def _(i, low=low, depth=depth):
            for odd in (0, 1):
                m = low + 2 * i + odd
                at = pl.ds(pl.multiple_of(m * ROWS, ROWS), ROWS)
                part = dot(turned[m, low:, :], work[at, :].astype(jnp.bfloat16))
                other = pltpu.roll(part, 2 * SLICE, 1)
                part = part.reshape(depth // 8, 8, LANES)
                other = other.reshape(depth // 8, 8, LANES) * sign
                full = part - other if odd else part + other
                rounded = full.reshape(depth, LANES).astype(jnp.bfloat16)
                values = rounded.astype(jnp.float32)
                left = pltpu.roll(values, LANES - SLICE, 1).reshape(depth // 8, 8, LANES)
                right = pltpu.roll(values, SLICE, 1).reshape(depth // 8, 8, LANES)
                turn = jnp.where(odd_group, right, -left).reshape(depth, LANES)
                spec[m, low:, :] = rounded
                swap[m, low:, :] = turn.astype(jnp.bfloat16)
                mixed = values * filt[0, low:, :] + turn * filt[1, low:, :]
                mixed = mixed.astype(jnp.bfloat16)
                if low:
                    mixed = jnp.concatenate(
                        [jnp.zeros((low, LANES), jnp.bfloat16), mixed], axis=0
                    )
                work[at, :] = dot(plain[m], mixed)

    @pl.loop(0, HALF)
    def _(j):
        modes = work[pl.ds(j, LANES, stride=ROWS), :].T.astype(jnp.bfloat16)
        cosine = jnp.concatenate(
            [modes[:SLICE], modes[2 * SLICE : 3 * SLICE]], axis=0
        )
        sine = jnp.concatenate([modes[SLICE : 2 * SLICE], modes[3 * SLICE :]], axis=0)
        signal = dot(cosine, inverse_ref[0]) + dot(sine, inverse_ref[1])
        slope[j] = gelu_slope(signal)

    for band in (2, 1, 0):
        arrive(cot, recv_c, band)
        arrive(cot, recv_c, PARTS - 1 - band)

        @pl.loop(0, BAND)
        def _(t, band=band):
            j = band * BAND + t
            north = cot[j].astype(jnp.float32) * slope[j, :SLICE]
            south = cot[NLAT - 1 - j].astype(jnp.float32) * slope[j, SLICE:]
            to_modes(
                north.astype(jnp.bfloat16),
                south.astype(jnp.bfloat16),
                inverse_ref,
                j,
                None,
            )

    acc[...] = jnp.zeros_like(acc)
    for group in range(8):
        low = 16 * group
        pairs = (min(16, MODES - low)) // 2

        @pl.loop(0, pairs)
        def _(i, low=low):
            total = [acc[0, low:, :], acc[1, low:, :]]
            for odd in (0, 1):
                m = low + 2 * i + odd
                at = pl.ds(pl.multiple_of(m * ROWS, ROWS), ROWS)
                back = dot(turned[m, low:, :], work[at, :].astype(jnp.bfloat16))
                total[0] += back * spec[m, low:, :].astype(jnp.float32)
                total[1] += back * swap[m, low:, :].astype(jnp.float32)
            acc[0, low:, :] = total[0]
            acc[1, low:, :] = total[1]

    for index in range(2):
        total = acc[index].T * scale
        packed[pl.ds(index * SLICE, SLICE), :] = (
            total[:SLICE] + total[SLICE : 2 * SLICE]
        ) + (total[2 * SLICE : 3 * SLICE] + total[3 * SLICE :])

    def remote(src, dst, send, recv, target):
        copy = pltpu.make_async_remote_copy(
            src_ref=src,
            dst_ref=dst,
            send_sem=send,
            recv_sem=recv,
            device_id=target,
            device_id_type=MESH,
        )
        copy.start()
        return copy

    def piece(x):
        return pl.ds(pl.multiple_of(x * rows, rows), rows)

    copies = [
        remote(packed.at[piece(x)], xbuf.at[xi], send_x.at[r], recv_x.at[r], at_x(x))
        for r, x in enumerate(x_peers)
    ]
    xbuf[xi] = packed[piece(xi), :]
    for copy in copies:
        copy.wait()
    mine[0] = sum((xbuf[i] for i in range(1, n_x)), xbuf[0])

    copies = [
        remote(mine.at[0], ybuf.at[yi], send_y.at[r], recv_y.at[r], at_y(y))
        for r, y in enumerate(y_peers)
    ]
    ybuf[yi] = mine[0]
    for copy in copies:
        copy.wait()
    mine[1] = sum((ybuf[i] for i in range(1, n_y)), ybuf[0])

    copies = [
        remote(mine.at[1], zbuf.at[zi], send_z.at[r], recv_z.at[r], at_z(z))
        for r, z in enumerate(z_peers)
    ]
    zbuf[zi] = mine[1]
    for copy in copies:
        copy.wait()
    mine[2] = sum((zbuf[i] for i in range(1, n_z)), zbuf[0])

    spot = gathered.at[me, piece(xi)]
    copies = [
        remote(mine.at[2], spot, send_s.at[r], recv_s.at[me], {"space": s})
        for r, s in enumerate(space_peers)
    ]
    gathered[me, piece(xi)] = mine[2]
    for copy in copies:
        copy.wait_send()
    for s in space_peers:
        spot = gathered.at[s, piece(xi)]
        pltpu.make_async_copy(spot, spot, recv_s.at[s]).wait()

    column = gathered.at[:, piece(xi)]
    copies = [
        remote(column, column, send_g.at[r], recv_g.at[xi], at_x(x))
        for r, x in enumerate(x_peers)
    ]
    for copy in copies:
        copy.wait_send()
    for x in x_peers:
        spot = gathered.at[:, piece(x)]
        pltpu.make_async_copy(spot, spot, recv_g.at[x]).wait()

    for s in range(PARTS):
        out_real[s * SLICE : (s + 1) * SLICE, :] = gathered[s, :SLICE, :MODES]
        out_imag[s * SLICE : (s + 1) * SLICE, :] = gathered[s, SLICE:, :MODES]
    for copy in sends:
        copy.wait_send()


def on_device(grid_dims, batch, fields, cotangent, spec_real, spec_imag):
    n_z, n_x, n_y = grid_dims
    rows = ROWS // n_x
    weight, plain, forward, inverse = tables()
    fields = jnp.transpose(fields[0], (0, 2, 1))
    cotangent = jnp.transpose(cotangent[0], (0, 2, 1))
    vmem = pl.BlockSpec(memory_space=pltpu.VMEM)
    anywhere = pl.BlockSpec(memory_space=pl.ANY)
    out = jax.ShapeDtypeStruct((CHANNELS, MODES), jnp.float32)
    dma = pltpu.SemaphoreType.DMA
    result = pl.pallas_call(
        functools.partial(kernel, grid_dims, 1.0 / batch),
        out_shape=(out, out),
        in_specs=[
            pl.BlockSpec(memory_space=pltpu.SMEM),
            anywhere,
            anywhere,
            anywhere,
            vmem,
            vmem,
            vmem,
            vmem,
        ],
        out_specs=(vmem, vmem),
        scratch_shapes=[
            pltpu.VMEM((NLAT, SLICE, NLON), jnp.bfloat16),
            pltpu.VMEM((NLAT, SLICE, NLON), jnp.bfloat16),
            pltpu.VMEM((MODES, ROWS, LANES), jnp.bfloat16),
            pltpu.VMEM((MODES, LANES, ROWS), jnp.bfloat16),
            pltpu.VMEM((LANES * ROWS, LANES), jnp.float32),
            pltpu.VMEM((HALF, ROWS, NLON), jnp.float32),
            pltpu.VMEM((MODES, LANES, LANES), jnp.bfloat16),
            pltpu.VMEM((MODES, LANES, LANES), jnp.bfloat16),
            pltpu.VMEM((2, LANES, LANES), jnp.float32),
            pltpu.VMEM((2, LANES, LANES), jnp.float32),
            pltpu.VMEM((ROWS, LANES), jnp.float32),
            pltpu.VMEM((n_x, rows, LANES), jnp.float32),
            pltpu.VMEM((n_y, rows, LANES), jnp.float32),
            pltpu.VMEM((n_z, rows, LANES), jnp.float32),
            pltpu.VMEM((3, rows, LANES), jnp.float32),
            pltpu.VMEM((PARTS, ROWS, LANES), jnp.float32),
            dma((1,)),
            dma((PARTS,)),
            dma((PARTS,)),
            dma((PARTS,)),
            dma((PARTS,)),
            dma((n_x,)),
            dma((n_x,)),
            dma((n_y,)),
            dma((n_y,)),
            dma((n_z,)),
            dma((n_z,)),
            dma((PARTS,)),
            dma((PARTS,)),
            dma((n_x,)),
            dma((n_x,)),
        ],
        compiler_params=pltpu.CompilerParams(
            collective_id=0, has_side_effects=True, vmem_limit_bytes=56 * 2**20
        ),
    )(
        jnp.asarray(weight),
        fields,
        cotangent,
        jnp.asarray(plain),
        jnp.asarray(forward),
        jnp.asarray(inverse),
        spec_real.T,
        spec_imag.T,
    )
    return (result[0].T, result[1].T)


def solution(mesh):
    samples = mesh.shape["dp"]
    grid_dims = (4, 4, 8) if samples == 128 else (1, 1, 1)
    in_specs = (P("dp", "space", None, None), P("dp", "space", None, None), P(), P())
    return jax.shard_map(
        functools.partial(on_device, grid_dims, samples),
        mesh=mesh,
        in_specs=in_specs,
        out_specs=(P(), P()),
        check_vma=False,
    )
```

```python
import functools
import math

import jax
import jax.numpy as jnp
import ml_dtypes
import numpy as np
from jax import lax
from jax.experimental import pallas as pl
from jax.experimental.pallas import tpu as pltpu
from jax.sharding import PartitionSpec as P

NLAT = 126
NLON = 252
MODES = 126
ORDERS = 128
CHANNELS = 192
HALF = 63
PARTS = 6
BAND = 21
SLICE = 32
ROWS = 64
LANES = 128
STEP = 3
UNROLL = 4
BACK_UNROLL = 8
MESH = pl.DeviceIdType.MESH
NT = (((1,), (1,)), ((), ()))
NN = (((1,), (0,)), ((), ()))


def legendre_table(theta):
    counters = np.arange(1, MODES, dtype=np.float64)
    steps = 0.5 * np.log((2.0 * counters + 1.0) / (2.0 * counters))
    log_table = np.concatenate([np.zeros(1), np.cumsum(steps)])
    orders = np.arange(MODES, dtype=np.float64)[:, None]
    diagonal = np.exp(
        0.5 * np.log(1.0 / (4.0 * math.pi))
        + log_table[:, None]
        + orders * np.log(np.sin(theta))[None, :]
    )
    cosine = np.cos(theta)[None, :]
    previous = np.zeros_like(diagonal)
    earlier = np.zeros_like(diagonal)
    table = np.zeros((MODES, MODES, theta.size))
    for degree in range(MODES):
        growth = np.sqrt(
            max(4.0 * degree * degree - 1.0, 0.0)
            / np.maximum(degree * degree - orders * orders, 1.0)
        )
        below = degree - 1.0
        damping = np.sqrt(
            np.maximum(below * below - orders * orders, 0.0)
            / max(4.0 * below * below - 1.0, 1.0)
        )
        current = growth * (cosine * previous - damping * earlier)
        current = np.where(
            orders == degree, diagonal, np.where(orders < degree, current, 0.0)
        )
        table[:, degree] = current
        previous, earlier = current, previous
    return table


def tables():
    theta = math.pi * (np.arange(HALF) + 0.5) / NLAT
    weight = np.zeros(ROWS, np.float32)
    weight[:HALF] = math.pi / NLAT * (2.0 * math.pi / NLON) * np.sin(theta)
    plain = np.zeros((ORDERS, ROWS, LANES), np.float32)
    plain[:MODES, :HALF, :MODES] = legendre_table(theta).transpose(0, 2, 1)
    orders = np.arange(MODES)
    phase = orders[:, None] * np.arange(NLON)[None, :] % NLON
    angles = 2.0 * math.pi / NLON * phase
    basis = np.zeros((2, LANES, NLON), np.float32)
    basis[0, :MODES] = np.cos(angles)
    basis[1, :MODES] = -np.sin(angles)
    factor = np.full((LANES, 1), 2.0, np.float32)
    factor[0] = 1.0
    forward = basis.astype(ml_dtypes.bfloat16)
    inverse = (forward.astype(np.float32) * factor).astype(ml_dtypes.bfloat16)
    return weight, plain.astype(ml_dtypes.bfloat16), forward, inverse


def gelu_slope(values):
    cumulative = 0.5 * (1.0 + lax.erf(values * (1.0 / math.sqrt(2.0))))
    density = jnp.exp(-0.5 * values * values) * (1.0 / math.sqrt(2.0 * math.pi))
    return cumulative + values * density


def dot(a, b, dims=NN):
    return lax.dot_general(a, b, dims, preferred_element_type=jnp.float32)


def kernel(
    grid_dims,
    weight_ref,
    fields_ref,
    cot_ref,
    plain_hbm,
    forward_hbm,
    inverse_hbm,
    real_ref,
    imag_ref,
    out_ref,
    field,
    cot,
    plain,
    forward_ref,
    inverse_ref,
    turned,
    work,
    back_work,
    slope,
    spec,
    swap,
    filt,
    mixes,
    acc,
    packed,
    xbuf,
    ybuf,
    zbuf,
    mine,
    gathered,
    local_sem,
    send_f,
    recv_f,
    send_c,
    recv_c,
    send_x,
    recv_x,
    send_y,
    recv_y,
    send_z,
    recv_z,
    send_s,
    recv_s,
    send_g,
    recv_g,
):
    n_z, n_x, n_y = grid_dims
    rows = ROWS // n_x
    me = lax.axis_index("space")
    dp = lax.axis_index("dp")
    zi = dp // (n_x * n_y)
    xi = lax.rem(dp // n_y, n_x)
    yi = lax.rem(dp, n_y)
    chip, core = me // 2, lax.rem(me, 2)
    first = jnp.where(chip == 0, 2, 0)
    second = 3 - chip - first
    space_peers = [
        2 * first + core,
        2 * first + 1 - core,
        2 * second + core,
        2 * second + 1 - core,
        2 * chip + 1 - core,
    ]
    x_peers = [lax.rem(xi + r, n_x) for r in range(1, n_x)]
    y_peers = [lax.rem(yi + r, n_y) for r in range(1, n_y)]
    z_peers = [lax.rem(zi + r, n_z) for r in range(1, n_z)]

    def at_x(x):
        return {"dp": (zi * n_x + x) * n_y + yi}

    def at_y(y):
        return {"dp": (zi * n_x + xi) * n_y + y}

    def at_z(z):
        return {"dp": (z * n_x + xi) * n_y + yi}

    everyone = (
        [{"space": s} for s in space_peers]
        + [at_x(x) for x in x_peers]
        + [at_y(y) for y in y_peers]
        + [at_z(z) for z in z_peers]
    )
    barrier = pltpu.get_barrier_semaphore()
    for target in everyone:
        pl.semaphore_signal(barrier, inc=1, device_id=target, device_id_type=MESH)

    loads = [
        pltpu.make_async_copy(source, target, local_sem.at[index])
        for index, (source, target) in enumerate(
            (
                (plain_hbm, plain),
                (forward_hbm, forward_ref),
                (inverse_hbm, inverse_ref),
            )
        )
    ]
    for load in loads:
        load.start()
    mine_lanes = pl.ds(pl.multiple_of(me * SLICE, SLICE), SLICE)
    own_f = pltpu.make_async_copy(
        fields_ref.at[:, mine_lanes, :], field.at[pl.ds(me * BAND, BAND)], recv_f.at[me]
    )
    own_c = pltpu.make_async_copy(
        cot_ref.at[:, mine_lanes, :], cot.at[pl.ds(me * BAND, BAND)], recv_c.at[me]
    )
    own_f.start()
    own_c.start()
    pl.semaphore_wait(barrier, len(everyone))

    def exchange(source, target, send, recv):
        copies = []
        for slot, peer in enumerate(space_peers):
            lanes = pl.ds(pl.multiple_of(peer * SLICE, SLICE), SLICE)
            copies.append(
                pltpu.make_async_remote_copy(
                    src_ref=source.at[:, lanes, :],
                    dst_ref=target.at[pl.ds(me * BAND, BAND)],
                    send_sem=send.at[slot],
                    recv_sem=recv.at[me],
                    device_id={"space": peer},
                    device_id_type=MESH,
                )
            )
            copies[-1].start()
        return copies

    sends = exchange(fields_ref, field, send_f, recv_f)
    sends += exchange(cot_ref, cot, send_c, recv_c)

    def arrive(target, recv, band):
        block = target.at[pl.ds(band * BAND, BAND)]
        pltpu.make_async_copy(block, block, recv.at[band]).wait()

    lane = lax.broadcasted_iota(jnp.int32, (LANES, LANES), 1)
    degree = lax.broadcasted_iota(jnp.int32, (LANES, LANES), 0)
    even_row = lax.rem(degree, 2) == lane // ROWS
    for index, source in enumerate((real_ref, imag_ref)):
        acc[index] = jnp.zeros((LANES, LANES), jnp.float32)
        values = source[mine_lanes, :].astype(jnp.float32)
        acc[index, :, :MODES] = jnp.concatenate([values] * 4, axis=0)
        values = acc[index].T
        filt[0, index] = jnp.where(even_row, values, 0.0)
        filt[1, index] = jnp.where(even_row, 0.0, values)
    mixes[...] = jnp.zeros_like(mixes)
    work[pl.ds(HALF, LANES, stride=ROWS), :] = jnp.zeros((LANES, LANES), jnp.float32)
    for load in loads:
        load.wait()

    @pl.loop(0, ORDERS // 4)
    def _(i):
        for index in range(4):
            turned[4 * i + index] = (
                plain[4 * i + index].astype(jnp.float32).T.astype(jnp.bfloat16)
            )

    zero = jnp.zeros((SLICE, NLON), jnp.bfloat16)

    def to_modes(pairs, basis_ref, first, factors):
        cosine = []
        sine = []
        for north, south in pairs:
            even = (north + south).astype(jnp.bfloat16)
            odd = (north - south).astype(jnp.bfloat16)
            cosine += [even, zero, odd, zero]
            sine += [zero, even, zero, odd]
        modes = dot(basis_ref[0], jnp.concatenate(cosine, axis=0), NT)
        modes += dot(basis_ref[1], jnp.concatenate(sine, axis=0), NT)
        for index in range(len(pairs)):
            part = modes[:, index * LANES : (index + 1) * LANES]
            if factors is not None:
                part = part * factors[index]
            work[pl.ds(first + index, LANES, stride=ROWS), :] = part

    for band in (2, 1, 0):
        arrive(field, recv_f, band)
        arrive(field, recv_f, PARTS - 1 - band)

        @pl.loop(0, BAND // STEP)
        def _(t, band=band):
            first = band * BAND + t * STEP
            js = [first + index for index in range(STEP)]
            to_modes(
                [
                    (
                        field[j].astype(jnp.float32),
                        field[NLAT - 1 - j].astype(jnp.float32),
                    )
                    for j in js
                ],
                forward_ref,
                first,
                [weight_ref[j] for j in js],
            )

    odd_group = lax.rem(lane[:ROWS] // SLICE, 2) == 1

    def rows_of(m):
        return pl.ds(pl.multiple_of(m * ROWS, ROWS), ROWS)

    def synthesize(m, index):
        back_work[rows_of(m), :] = dot(plain[m], mixes[index])

    for low in range(0, ORDERS, 16):

        @pl.loop(0, 16 // UNROLL)
        def _(i, low=low):
            start = low + UNROLL * i
            for index in range(UNROLL):
                synthesize(jnp.maximum(start - UNROLL, 0) + index, index)
            for index in range(UNROLL):
                m = start + index
                modes = work[rows_of(m), :]
                turn = jnp.where(
                    odd_group,
                    pltpu.roll(modes, SLICE, 1),
                    -pltpu.roll(modes, LANES - SLICE, 1),
                )
                both = jnp.concatenate([modes, turn], axis=1).astype(jnp.bfloat16)
                full = dot(turned[m, low:, :], both)
                values, turn = full[:, :LANES], full[:, LANES:]
                spec[m, low:, :] = values.astype(jnp.bfloat16)
                swap[m, low:, :] = turn.astype(jnp.bfloat16)
                parity = index % 2
                mixed = values * filt[parity, 0, low:, :] + turn * filt[parity, 1, low:, :]
                mixed = mixed.astype(jnp.bfloat16)
                if low:
                    mixed = jnp.concatenate(
                        [jnp.zeros((low, LANES), jnp.bfloat16), mixed], axis=0
                    )
                mixes[index] = mixed

    for index in range(UNROLL):
        synthesize(ORDERS - UNROLL + index, index)

    @pl.loop(0, HALF // STEP)
    def _(t):
        for index in range(STEP):
            j = t * STEP + index
            modes = back_work[pl.ds(j, LANES, stride=ROWS), :].T
            north = (modes[:ROWS] + modes[ROWS:]).astype(jnp.bfloat16)
            south = (modes[:ROWS] - modes[ROWS:]).astype(jnp.bfloat16)
            cosine = jnp.concatenate([north[:SLICE], south[:SLICE]], axis=0)
            sine = jnp.concatenate([north[SLICE:], south[SLICE:]], axis=0)
            signal = dot(
                jnp.concatenate([cosine, sine], axis=1),
                inverse_ref[...].reshape(2 * LANES, NLON),
            )
            slope[j] = gelu_slope(signal)

    for band in (2, 1, 0):
        arrive(cot, recv_c, band)
        arrive(cot, recv_c, PARTS - 1 - band)

        @pl.loop(0, BAND // STEP)
        def _(t, band=band):
            first = band * BAND + t * STEP
            pairs = []
            for index in range(STEP):
                j = first + index
                north = cot[j].astype(jnp.float32) * slope[j, :SLICE]
                south = cot[NLAT - 1 - j].astype(jnp.float32) * slope[j, SLICE:]
                pairs.append((north, south))
            to_modes(pairs, inverse_ref, first, None)

    acc[...] = jnp.zeros_like(acc)
    for low in range(0, ORDERS, 16):

        @pl.loop(0, 16 // BACK_UNROLL)
        def _(i, low=low):
            total = [acc[index, low:, :] for index in range(4)]
            for index in range(BACK_UNROLL):
                m = low + BACK_UNROLL * i + index
                parity = index % 2
                back = dot(turned[m, low:, :], work[rows_of(m), :].astype(jnp.bfloat16))
                total[parity] += back * spec[m, low:, :].astype(jnp.float32)
                total[2 + parity] += back * swap[m, low:, :].astype(jnp.float32)
            for index in range(4):
                acc[index, low:, :] = total[index]

    for index in range(2):
        total = jnp.where(even_row, acc[2 * index], acc[2 * index + 1]).T
        packed[pl.ds(index * SLICE, SLICE), :] = (
            total[:SLICE] + total[SLICE : 2 * SLICE]
        ) + (total[2 * SLICE : 3 * SLICE] + total[3 * SLICE :])

    def remote(src, dst, send, recv, target):
        copy = pltpu.make_async_remote_copy(
            src_ref=src,
            dst_ref=dst,
            send_sem=send,
            recv_sem=recv,
            device_id=target,
            device_id_type=MESH,
        )
        copy.start()
        return copy

    def piece(x):
        return pl.ds(pl.multiple_of(x * rows, rows), rows)

    copies = [
        remote(packed.at[piece(x)], xbuf.at[xi], send_x.at[r], recv_x.at[r], at_x(x))
        for r, x in enumerate(x_peers)
    ]
    xbuf[xi] = packed[piece(xi), :]
    for copy in copies:
        copy.wait()
    mine[0] = sum((xbuf[i] for i in range(1, n_x)), xbuf[0])

    copies = [
        remote(mine.at[0], ybuf.at[yi], send_y.at[r], recv_y.at[r], at_y(y))
        for r, y in enumerate(y_peers)
    ]
    ybuf[yi] = mine[0]
    for copy in copies:
        copy.wait()
    mine[1] = sum((ybuf[i] for i in range(1, n_y)), ybuf[0])

    copies = [
        remote(mine.at[1], zbuf.at[zi], send_z.at[r], recv_z.at[r], at_z(z))
        for r, z in enumerate(z_peers)
    ]
    zbuf[zi] = mine[1]
    for copy in copies:
        copy.wait()
    mine[2] = sum((zbuf[i] for i in range(1, n_z)), zbuf[0])

    spot = gathered.at[me, piece(xi)]
    copies = [
        remote(mine.at[2], spot, send_s.at[r], recv_s.at[me], {"space": s})
        for r, s in enumerate(space_peers)
    ]
    gathered[me, piece(xi)] = mine[2]
    for copy in copies:
        copy.wait_send()
    for s in space_peers:
        spot = gathered.at[s, piece(xi)]
        pltpu.make_async_copy(spot, spot, recv_s.at[s]).wait()

    column = gathered.at[:, piece(xi)]
    copies = [
        remote(column, column, send_g.at[r], recv_g.at[xi], at_x(x))
        for r, x in enumerate(x_peers)
    ]
    for copy in copies:
        copy.wait_send()
    for x in x_peers:
        spot = gathered.at[:, piece(x)]
        pltpu.make_async_copy(spot, spot, recv_g.at[x]).wait()

    for s in range(PARTS):
        for index in range(2):
            out_ref[index, s * SLICE : (s + 1) * SLICE, :] = gathered[
                s, index * SLICE : (index + 1) * SLICE, :MODES
            ]
    for copy in sends:
        copy.wait_send()


def on_device(grid_dims, batch, fields, cotangent, spec_real, spec_imag):
    n_z, n_x, n_y = grid_dims
    rows = ROWS // n_x
    weight, plain, forward, inverse = tables()
    fields = jnp.transpose(fields[0], (0, 2, 1))
    cotangent = jnp.transpose(cotangent[0], (0, 2, 1))
    vmem = pl.BlockSpec(memory_space=pltpu.VMEM)
    anywhere = pl.BlockSpec(memory_space=pl.ANY)
    out = jax.ShapeDtypeStruct((2, CHANNELS, MODES), jnp.float32)
    dma = pltpu.SemaphoreType.DMA
    result = pl.pallas_call(
        functools.partial(kernel, grid_dims),
        out_shape=out,
        in_specs=[
            pl.BlockSpec(memory_space=pltpu.SMEM),
            anywhere,
            anywhere,
            anywhere,
            anywhere,
            anywhere,
            vmem,
            vmem,
        ],
        out_specs=vmem,
        scratch_shapes=[
            pltpu.VMEM((NLAT, SLICE, NLON), jnp.bfloat16),
            pltpu.VMEM((NLAT, SLICE, NLON), jnp.bfloat16),
            pltpu.VMEM((ORDERS, ROWS, LANES), jnp.bfloat16),
            pltpu.VMEM((2, LANES, NLON), jnp.bfloat16),
            pltpu.VMEM((2, LANES, NLON), jnp.bfloat16),
            pltpu.VMEM((ORDERS, LANES, ROWS), jnp.bfloat16),
            pltpu.VMEM((ORDERS * ROWS, LANES), jnp.float32),
            pltpu.VMEM((ORDERS * ROWS, LANES), jnp.float32),
            pltpu.VMEM((HALF, ROWS, NLON), jnp.float32),
            pltpu.VMEM((ORDERS, LANES, LANES), jnp.bfloat16),
            pltpu.VMEM((ORDERS, LANES, LANES), jnp.bfloat16),
            pltpu.VMEM((2, 2, LANES, LANES), jnp.float32),
            pltpu.VMEM((UNROLL, LANES, LANES), jnp.bfloat16),
            pltpu.VMEM((4, LANES, LANES), jnp.float32),
            pltpu.VMEM((ROWS, LANES), jnp.float32),
            pltpu.VMEM((n_x, rows, LANES), jnp.float32),
            pltpu.VMEM((n_y, rows, LANES), jnp.float32),
            pltpu.VMEM((n_z, rows, LANES), jnp.float32),
            pltpu.VMEM((3, rows, LANES), jnp.float32),
            pltpu.VMEM((PARTS, ROWS, LANES), jnp.float32),
            dma((3,)),
            dma((PARTS,)),
            dma((PARTS,)),
            dma((PARTS,)),
            dma((PARTS,)),
            dma((n_x,)),
            dma((n_x,)),
            dma((n_y,)),
            dma((n_y,)),
            dma((n_z,)),
            dma((n_z,)),
            dma((PARTS,)),
            dma((PARTS,)),
            dma((n_x,)),
            dma((n_x,)),
        ],
        compiler_params=pltpu.CompilerParams(
            collective_id=0, has_side_effects=True, vmem_limit_bytes=56 * 2**20
        ),
    )(
        jnp.asarray(weight),
        fields,
        cotangent,
        jnp.asarray(plain),
        jnp.asarray(forward),
        jnp.asarray(inverse),
        spec_real.T,
        spec_imag.T,
    )
    result = result * (1.0 / batch)
    return (result[0].T, result[1].T)


def solution(mesh):
    samples = mesh.shape["dp"]
    grid_dims = (4, 4, 8) if samples == 128 else (1, 1, 1)
    in_specs = (P("dp", "space", None, None), P("dp", "space", None, None), P(), P())
    return jax.shard_map(
        functools.partial(on_device, grid_dims, samples),
        mesh=mesh,
        in_specs=in_specs,
        out_specs=(P(), P()),
        check_vma=False,
    )
```

```python
import functools
import math

import jax
import jax.numpy as jnp
import ml_dtypes
import numpy as np
from jax import lax
from jax.experimental import pallas as pl
from jax.experimental.pallas import tpu as pltpu
from jax.sharding import PartitionSpec as P

NLAT = 126
NLON = 252
MODES = 126
ORDERS = 128
CHANNELS = 192
HALF = 63
PARTS = 6
BAND = 21
SLICE = 32
ROWS = 64
LANES = 128
STEP = 3
UNROLL = 4
BACK_UNROLL = 8
MESH = pl.DeviceIdType.MESH
NT = (((1,), (1,)), ((), ()))
NN = (((1,), (0,)), ((), ()))


def legendre_table(theta):
    counters = np.arange(1, MODES, dtype=np.float64)
    steps = 0.5 * np.log((2.0 * counters + 1.0) / (2.0 * counters))
    log_table = np.concatenate([np.zeros(1), np.cumsum(steps)])
    orders = np.arange(MODES, dtype=np.float64)[:, None]
    diagonal = np.exp(
        0.5 * np.log(1.0 / (4.0 * math.pi))
        + log_table[:, None]
        + orders * np.log(np.sin(theta))[None, :]
    )
    cosine = np.cos(theta)[None, :]
    previous = np.zeros_like(diagonal)
    earlier = np.zeros_like(diagonal)
    table = np.zeros((MODES, MODES, theta.size))
    for degree in range(MODES):
        growth = np.sqrt(
            max(4.0 * degree * degree - 1.0, 0.0)
            / np.maximum(degree * degree - orders * orders, 1.0)
        )
        below = degree - 1.0
        damping = np.sqrt(
            np.maximum(below * below - orders * orders, 0.0)
            / max(4.0 * below * below - 1.0, 1.0)
        )
        current = growth * (cosine * previous - damping * earlier)
        current = np.where(
            orders == degree, diagonal, np.where(orders < degree, current, 0.0)
        )
        table[:, degree] = current
        previous, earlier = current, previous
    return table


def tables():
    theta = math.pi * (np.arange(HALF) + 0.5) / NLAT
    weight = np.zeros((ROWS, LANES), np.float32)
    weight[:HALF] = (math.pi / NLAT * (2.0 * math.pi / NLON) * np.sin(theta))[:, None]
    plain = np.zeros((ORDERS, ROWS, LANES), np.float32)
    plain[:MODES, :HALF, :MODES] = legendre_table(theta).transpose(0, 2, 1)
    orders = np.arange(MODES)
    phase = orders[:, None] * np.arange(NLON)[None, :] % NLON
    angles = 2.0 * math.pi / NLON * phase
    basis = np.zeros((2, LANES, NLON), np.float32)
    basis[0, :MODES] = np.cos(angles)
    basis[1, :MODES] = -np.sin(angles)
    factor = np.full((LANES, 1), 2.0, np.float32)
    factor[0] = 1.0
    forward = basis.astype(ml_dtypes.bfloat16)
    inverse = (forward.astype(np.float32) * factor).astype(ml_dtypes.bfloat16)
    return weight, plain.astype(ml_dtypes.bfloat16), forward, inverse


def gelu_slope(values):
    cumulative = 0.5 * (1.0 + lax.erf(values * (1.0 / math.sqrt(2.0))))
    density = jnp.exp(-0.5 * values * values) * (1.0 / math.sqrt(2.0 * math.pi))
    return cumulative + values * density


def dot(a, b, dims=NN):
    return lax.dot_general(a, b, dims, preferred_element_type=jnp.float32)


def kernel(
    grid_dims,
    scale,
    weight_hbm,
    fields_ref,
    cot_ref,
    plain_hbm,
    forward_hbm,
    inverse_hbm,
    real_hbm,
    imag_hbm,
    out_ref,
    field,
    cot,
    plain,
    forward_ref,
    inverse_ref,
    weight_ref,
    real_ref,
    imag_ref,
    turned,
    work,
    back_work,
    slope,
    spec,
    swap,
    filt,
    mixes,
    acc,
    packed,
    xbuf,
    ybuf,
    zbuf,
    mine,
    gathered,
    local_sem,
    send_f,
    recv_f,
    send_c,
    recv_c,
    send_x,
    recv_x,
    send_y,
    recv_y,
    send_z,
    recv_z,
    send_s,
    recv_s,
    send_g,
    recv_g,
):
    n_z, n_x, n_y = grid_dims
    rows = ROWS // n_x
    me = lax.axis_index("space")
    dp = lax.axis_index("dp")
    zi = dp // (n_x * n_y)
    xi = lax.rem(dp // n_y, n_x)
    yi = lax.rem(dp, n_y)
    chip, core = me // 2, lax.rem(me, 2)
    near = jnp.where(chip == 1, 0, 1)
    far = 3 - chip - near
    space_peers = [
        2 * chip + 1 - core,
        2 * near + core,
        2 * near + 1 - core,
        2 * far + core,
        2 * far + 1 - core,
    ]
    second = jnp.where(chip == 0, 1 - core, jnp.where(chip == 2, core, 1))

    def band_of(turn):
        return jnp.where(turn == 0, 2, jnp.where(turn == 1, second, 1 - second))

    x_peers = [lax.rem(xi + r, n_x) for r in range(1, n_x)]
    y_peers = [lax.rem(yi + r, n_y) for r in range(1, n_y)]
    z_peers = [lax.rem(zi + r, n_z) for r in range(1, n_z)]

    def at_x(x):
        return {"dp": (zi * n_x + x) * n_y + yi}

    def at_y(y):
        return {"dp": (zi * n_x + xi) * n_y + y}

    def at_z(z):
        return {"dp": (z * n_x + xi) * n_y + yi}

    everyone = (
        [{"space": s} for s in space_peers]
        + [at_x(x) for x in x_peers]
        + [at_y(y) for y in y_peers]
        + [at_z(z) for z in z_peers]
    )
    barrier = pltpu.get_barrier_semaphore()
    for target in everyone:
        pl.semaphore_signal(barrier, inc=1, device_id=target, device_id_type=MESH)

    loads = [
        pltpu.make_async_copy(source, target, local_sem.at[index])
        for index, (source, target) in enumerate(
            (
                (plain_hbm, plain),
                (forward_hbm, forward_ref),
                (inverse_hbm, inverse_ref),
                (weight_hbm, weight_ref),
                (real_hbm, real_ref),
                (imag_hbm, imag_ref),
            )
        )
    ]
    for load in loads:
        load.start()
    mine_lanes = pl.ds(pl.multiple_of(me * SLICE, SLICE), SLICE)
    own_f = pltpu.make_async_copy(
        fields_ref.at[:, mine_lanes, :], field.at[pl.ds(me * BAND, BAND)], recv_f.at[me]
    )
    own_c = pltpu.make_async_copy(
        cot_ref.at[:, mine_lanes, :], cot.at[pl.ds(me * BAND, BAND)], recv_c.at[me]
    )
    own_f.start()
    own_c.start()
    pl.semaphore_wait(barrier, len(everyone))

    def exchange(source, target, send, recv):
        copies = []
        for slot, peer in enumerate(space_peers):
            lanes = pl.ds(pl.multiple_of(peer * SLICE, SLICE), SLICE)
            copies.append(
                pltpu.make_async_remote_copy(
                    src_ref=source.at[:, lanes, :],
                    dst_ref=target.at[pl.ds(me * BAND, BAND)],
                    send_sem=send.at[slot],
                    recv_sem=recv.at[me],
                    device_id={"space": peer},
                    device_id_type=MESH,
                )
            )
            copies[-1].start()
        return copies

    sends = exchange(fields_ref, field, send_f, recv_f)
    sends += exchange(cot_ref, cot, send_c, recv_c)

    def arrive(target, recv, band):
        block = target.at[pl.ds(band * BAND, BAND)]
        pltpu.make_async_copy(block, block, recv.at[band]).wait()

    for load in loads:
        load.wait()

    lane = lax.broadcasted_iota(jnp.int32, (LANES, LANES), 1)
    degree = lax.broadcasted_iota(jnp.int32, (LANES, LANES), 0)
    even_row = lax.rem(degree, 2) == lane // ROWS
    for index, source in enumerate((real_ref, imag_ref)):
        acc[index] = jnp.zeros((LANES, LANES), jnp.float32)
        values = source[mine_lanes, :].astype(jnp.float32)
        acc[index, :, :MODES] = jnp.concatenate([values] * 4, axis=0)
        values = acc[index].T
        filt[0, index] = jnp.where(even_row, values, 0.0)
        filt[1, index] = jnp.where(even_row, 0.0, values)
    mixes[...] = jnp.zeros_like(mixes)
    work[pl.ds(HALF, LANES, stride=ROWS), :] = jnp.zeros((LANES, LANES), jnp.float32)
    @pl.loop(0, ORDERS // 4)
    def _(i):
        for index in range(4):
            turned[4 * i + index] = (
                plain[4 * i + index].astype(jnp.float32).T.astype(jnp.bfloat16)
            )

    zero = jnp.zeros((SLICE, NLON), jnp.bfloat16)

    def to_modes(pairs, basis_ref, first, factors):
        cosine = []
        sine = []
        for north, south in pairs:
            even = (north + south).astype(jnp.bfloat16)
            odd = (north - south).astype(jnp.bfloat16)
            cosine += [even, zero, odd, zero]
            sine += [zero, even, zero, odd]
        modes = dot(basis_ref[0], jnp.concatenate(cosine, axis=0), NT)
        modes += dot(basis_ref[1], jnp.concatenate(sine, axis=0), NT)
        for index in range(len(pairs)):
            part = modes[:, index * LANES : (index + 1) * LANES]
            if factors is not None:
                part = part * factors[index]
            work[pl.ds(first + index, LANES, stride=ROWS), :] = part

    @pl.loop(0, PARTS // 2)
    def _(turn):
        band = band_of(turn)
        arrive(field, recv_f, band)
        arrive(field, recv_f, PARTS - 1 - band)

        @pl.loop(0, BAND // STEP)
        def _(t):
            first = band * BAND + t * STEP
            js = [first + index for index in range(STEP)]
            to_modes(
                [
                    (
                        field[j].astype(jnp.float32),
                        field[NLAT - 1 - j].astype(jnp.float32),
                    )
                    for j in js
                ],
                forward_ref,
                first,
                [weight_ref[pl.ds(j, 1), :] for j in js],
            )

    odd_group = lax.rem(lane[:ROWS] // SLICE, 2) == 1

    def rows_of(m):
        return pl.ds(pl.multiple_of(m * ROWS, ROWS), ROWS)

    def synthesize(m, index):
        back_work[rows_of(m), :] = dot(plain[m], mixes[index])

    for low in range(0, ORDERS, 16):

        @pl.loop(0, 16 // UNROLL)
        def _(i, low=low):
            start = low + UNROLL * i
            for index in range(UNROLL):
                synthesize(jnp.maximum(start - UNROLL, 0) + index, index)
            for index in range(UNROLL):
                m = start + index
                modes = work[rows_of(m), :]
                turn = jnp.where(
                    odd_group,
                    pltpu.roll(modes, SLICE, 1),
                    -pltpu.roll(modes, LANES - SLICE, 1),
                )
                both = jnp.concatenate([modes, turn], axis=1).astype(jnp.bfloat16)
                full = dot(turned[m, low:, :], both)
                values, turn = full[:, :LANES], full[:, LANES:]
                spec[m, low:, :] = values.astype(jnp.bfloat16)
                swap[m, low:, :] = turn.astype(jnp.bfloat16)
                parity = index % 2
                mixed = values * filt[parity, 0, low:, :] + turn * filt[parity, 1, low:, :]
                mixed = mixed.astype(jnp.bfloat16)
                if low:
                    mixed = jnp.concatenate(
                        [jnp.zeros((low, LANES), jnp.bfloat16), mixed], axis=0
                    )
                mixes[index] = mixed

    for index in range(UNROLL):
        synthesize(ORDERS - UNROLL + index, index)

    @pl.loop(0, HALF // STEP)
    def _(t):
        for index in range(STEP):
            j = t * STEP + index
            modes = back_work[pl.ds(j, LANES, stride=ROWS), :].T
            north = (modes[:ROWS] + modes[ROWS:]).astype(jnp.bfloat16)
            south = (modes[:ROWS] - modes[ROWS:]).astype(jnp.bfloat16)
            cosine = jnp.concatenate([north[:SLICE], south[:SLICE]], axis=0)
            sine = jnp.concatenate([north[SLICE:], south[SLICE:]], axis=0)
            signal = dot(
                jnp.concatenate([cosine, sine], axis=1),
                inverse_ref[...].reshape(2 * LANES, NLON),
            )
            slope[j] = gelu_slope(signal)

    @pl.loop(0, PARTS // 2)
    def _(turn):
        band = band_of(turn)
        arrive(cot, recv_c, band)
        arrive(cot, recv_c, PARTS - 1 - band)

        @pl.loop(0, BAND // STEP)
        def _(t):
            first = band * BAND + t * STEP
            pairs = []
            for index in range(STEP):
                j = first + index
                north = cot[j].astype(jnp.float32) * slope[j, :SLICE]
                south = cot[NLAT - 1 - j].astype(jnp.float32) * slope[j, SLICE:]
                pairs.append((north, south))
            to_modes(pairs, inverse_ref, first, None)

    acc[...] = jnp.zeros_like(acc)
    for low in range(0, ORDERS, 16):

        @pl.loop(0, 16 // BACK_UNROLL)
        def _(i, low=low):
            total = [acc[index, low:, :] for index in range(4)]
            for index in range(BACK_UNROLL):
                m = low + BACK_UNROLL * i + index
                parity = index % 2
                back = dot(turned[m, low:, :], work[rows_of(m), :].astype(jnp.bfloat16))
                total[parity] += back * spec[m, low:, :].astype(jnp.float32)
                total[2 + parity] += back * swap[m, low:, :].astype(jnp.float32)
            for index in range(4):
                acc[index, low:, :] = total[index]

    for index in range(2):
        total = jnp.where(even_row, acc[2 * index], acc[2 * index + 1]).T * scale
        packed[pl.ds(index * SLICE, SLICE), :] = (
            total[:SLICE] + total[SLICE : 2 * SLICE]
        ) + (total[2 * SLICE : 3 * SLICE] + total[3 * SLICE :])

    def remote(src, dst, send, recv, target):
        copy = pltpu.make_async_remote_copy(
            src_ref=src,
            dst_ref=dst,
            send_sem=send,
            recv_sem=recv,
            device_id=target,
            device_id_type=MESH,
        )
        copy.start()
        return copy

    def piece(x):
        return pl.ds(pl.multiple_of(x * rows, rows), rows)

    copies = [
        remote(packed.at[piece(x)], xbuf.at[xi], send_x.at[r], recv_x.at[r], at_x(x))
        for r, x in enumerate(x_peers)
    ]
    xbuf[xi] = packed[piece(xi), :]
    for copy in copies:
        copy.wait()
    mine[0] = sum((xbuf[i] for i in range(1, n_x)), xbuf[0])

    copies = [
        remote(mine.at[0], ybuf.at[yi], send_y.at[r], recv_y.at[r], at_y(y))
        for r, y in enumerate(y_peers)
    ]
    ybuf[yi] = mine[0]
    for copy in copies:
        copy.wait()
    mine[1] = sum((ybuf[i] for i in range(1, n_y)), ybuf[0])

    copies = [
        remote(mine.at[1], zbuf.at[zi], send_z.at[r], recv_z.at[r], at_z(z))
        for r, z in enumerate(z_peers)
    ]
    zbuf[zi] = mine[1]
    for copy in copies:
        copy.wait()
    mine[2] = sum((zbuf[i] for i in range(1, n_z)), zbuf[0])

    spot = gathered.at[me, piece(xi)]
    copies = [
        remote(mine.at[2], spot, send_s.at[r], recv_s.at[me], {"space": s})
        for r, s in enumerate(space_peers)
    ]
    gathered[me, piece(xi)] = mine[2]
    for copy in copies:
        copy.wait_send()
    for s in space_peers:
        spot = gathered.at[s, piece(xi)]
        pltpu.make_async_copy(spot, spot, recv_s.at[s]).wait()

    column = gathered.at[:, piece(xi)]
    copies = [
        remote(column, column, send_g.at[r], recv_g.at[xi], at_x(x))
        for r, x in enumerate(x_peers)
    ]
    for copy in copies:
        copy.wait_send()
    for x in x_peers:
        spot = gathered.at[:, piece(x)]
        pltpu.make_async_copy(spot, spot, recv_g.at[x]).wait()

    for s in range(PARTS):
        for index in range(2):
            out_ref[index, s * SLICE : (s + 1) * SLICE, :] = gathered[
                s, index * SLICE : (index + 1) * SLICE, :MODES
            ]
    for copy in sends:
        copy.wait_send()


def on_device(grid_dims, batch, fields, cotangent, spec_real, spec_imag):
    n_z, n_x, n_y = grid_dims
    rows = ROWS // n_x
    weight, plain, forward, inverse = tables()
    fields = jnp.transpose(fields[0], (0, 2, 1))
    cotangent = jnp.transpose(cotangent[0], (0, 2, 1))
    vmem = pl.BlockSpec(memory_space=pltpu.VMEM)
    anywhere = pl.BlockSpec(memory_space=pl.ANY)
    out = jax.ShapeDtypeStruct((2, CHANNELS, MODES), jnp.float32)
    dma = pltpu.SemaphoreType.DMA
    result = pl.pallas_call(
        functools.partial(kernel, grid_dims, 1.0 / batch),
        out_shape=out,
        in_specs=[
            anywhere,
        ]
        * 8,
        out_specs=vmem,
        scratch_shapes=[
            pltpu.VMEM((NLAT, SLICE, NLON), jnp.bfloat16),
            pltpu.VMEM((NLAT, SLICE, NLON), jnp.bfloat16),
            pltpu.VMEM((ORDERS, ROWS, LANES), jnp.bfloat16),
            pltpu.VMEM((2, LANES, NLON), jnp.bfloat16),
            pltpu.VMEM((2, LANES, NLON), jnp.bfloat16),
            pltpu.VMEM((ROWS, LANES), jnp.float32),
            pltpu.VMEM((CHANNELS, MODES), jnp.bfloat16),
            pltpu.VMEM((CHANNELS, MODES), jnp.bfloat16),
            pltpu.VMEM((ORDERS, LANES, ROWS), jnp.bfloat16),
            pltpu.VMEM((ORDERS * ROWS, LANES), jnp.float32),
            pltpu.VMEM((ORDERS * ROWS, LANES), jnp.float32),
            pltpu.VMEM((HALF, ROWS, NLON), jnp.float32),
            pltpu.VMEM((ORDERS, LANES, LANES), jnp.bfloat16),
            pltpu.VMEM((ORDERS, LANES, LANES), jnp.bfloat16),
            pltpu.VMEM((2, 2, LANES, LANES), jnp.float32),
            pltpu.VMEM((UNROLL, LANES, LANES), jnp.bfloat16),
            pltpu.VMEM((4, LANES, LANES), jnp.float32),
            pltpu.VMEM((ROWS, LANES), jnp.float32),
            pltpu.VMEM((n_x, rows, LANES), jnp.float32),
            pltpu.VMEM((n_y, rows, LANES), jnp.float32),
            pltpu.VMEM((n_z, rows, LANES), jnp.float32),
            pltpu.VMEM((3, rows, LANES), jnp.float32),
            pltpu.VMEM((PARTS, ROWS, LANES), jnp.float32),
            dma((6,)),
            dma((PARTS,)),
            dma((PARTS,)),
            dma((PARTS,)),
            dma((PARTS,)),
            dma((n_x,)),
            dma((n_x,)),
            dma((n_y,)),
            dma((n_y,)),
            dma((n_z,)),
            dma((n_z,)),
            dma((PARTS,)),
            dma((PARTS,)),
            dma((n_x,)),
            dma((n_x,)),
        ],
        compiler_params=pltpu.CompilerParams(
            collective_id=0, has_side_effects=True, vmem_limit_bytes=56 * 2**20
        ),
    )(
        jnp.asarray(weight),
        fields,
        cotangent,
        jnp.asarray(plain),
        jnp.asarray(forward),
        jnp.asarray(inverse),
        spec_real.T,
        spec_imag.T,
    )
    return (result[0].T, result[1].T)


def solution(mesh):
    samples = mesh.shape["dp"]
    grid_dims = (4, 4, 8) if samples == 128 else (1, 1, 1)
    in_specs = (P("dp", "space", None, None), P("dp", "space", None, None), P(), P())
    return jax.shard_map(
        functools.partial(on_device, grid_dims, samples),
        mesh=mesh,
        in_specs=in_specs,
        out_specs=(P(), P()),
        check_vma=False,
    )
```

```python
import functools
import math

import jax
import jax.numpy as jnp
import ml_dtypes
import numpy as np
from jax import lax
from jax.experimental import pallas as pl
from jax.experimental.pallas import tpu as pltpu
from jax.sharding import PartitionSpec as P

NLAT = 126
NLON = 252
MODES = 126
ORDERS = 128
CHANNELS = 192
HALF = 63
PARTS = 6
BAND = 21
SLICE = 32
ROWS = 64
LANES = 128
STEP = 3
PIECES = ((0, 9), (9, 6), (15, 6))
UNROLL = 4
BACK_UNROLL = 16
DEGREES = 64
MESH = pl.DeviceIdType.MESH
NT = (((1,), (1,)), ((), ()))
NN = (((1,), (0,)), ((), ()))


def legendre_table(theta):
    counters = np.arange(1, MODES, dtype=np.float64)
    steps = 0.5 * np.log((2.0 * counters + 1.0) / (2.0 * counters))
    log_table = np.concatenate([np.zeros(1), np.cumsum(steps)])
    orders = np.arange(MODES, dtype=np.float64)[:, None]
    diagonal = np.exp(
        0.5 * np.log(1.0 / (4.0 * math.pi))
        + log_table[:, None]
        + orders * np.log(np.sin(theta))[None, :]
    )
    cosine = np.cos(theta)[None, :]
    previous = np.zeros_like(diagonal)
    earlier = np.zeros_like(diagonal)
    table = np.zeros((MODES, MODES, theta.size))
    for degree in range(MODES):
        growth = np.sqrt(
            max(4.0 * degree * degree - 1.0, 0.0)
            / np.maximum(degree * degree - orders * orders, 1.0)
        )
        below = degree - 1.0
        damping = np.sqrt(
            np.maximum(below * below - orders * orders, 0.0)
            / max(4.0 * below * below - 1.0, 1.0)
        )
        current = growth * (cosine * previous - damping * earlier)
        current = np.where(
            orders == degree, diagonal, np.where(orders < degree, current, 0.0)
        )
        table[:, degree] = current
        previous, earlier = current, previous
    return table


def tables():
    theta = math.pi * (np.arange(HALF) + 0.5) / NLAT
    weight = np.zeros((ROWS, LANES), np.float32)
    weight[:HALF] = (math.pi / NLAT * (2.0 * math.pi / NLON) * np.sin(theta))[:, None]
    plain = np.zeros((ORDERS, ROWS, LANES), np.float32)
    plain[:MODES, :HALF, :MODES] = legendre_table(theta).transpose(0, 2, 1)
    orders = np.arange(MODES)
    phase = orders[:, None] * np.arange(NLON)[None, :] % NLON
    angles = 2.0 * math.pi / NLON * phase
    basis = np.zeros((2, LANES, NLON), np.float32)
    basis[0, :MODES] = np.cos(angles)
    basis[1, :MODES] = -np.sin(angles)
    factor = np.full((LANES, 1), 2.0, np.float32)
    factor[0] = 1.0
    forward = basis.astype(ml_dtypes.bfloat16)
    inverse = (forward.astype(np.float32) * factor).astype(ml_dtypes.bfloat16)
    return weight, plain.astype(ml_dtypes.bfloat16), forward, inverse


def gelu_slope(values):
    cumulative = 0.5 * (1.0 + lax.erf(values * (1.0 / math.sqrt(2.0))))
    density = jnp.exp(-0.5 * values * values) * (1.0 / math.sqrt(2.0 * math.pi))
    return cumulative + values * density


def dot(a, b, dims=NN):
    return lax.dot_general(a, b, dims, preferred_element_type=jnp.float32)


def kernel(
    grid_dims,
    scale,
    weight_hbm,
    fields_ref,
    cot_ref,
    plain_hbm,
    forward_hbm,
    inverse_hbm,
    real_hbm,
    imag_hbm,
    out_ref,
    field,
    cot,
    plain,
    forward_ref,
    inverse_ref,
    weight_ref,
    real_ref,
    imag_ref,
    turned,
    work,
    back_work,
    slope,
    spec,
    swap,
    filt,
    mixes,
    acc,
    packed,
    xbuf,
    ybuf,
    zbuf,
    mine,
    gathered,
    local_sem,
    send_f,
    recv_f,
    send_c,
    recv_c,
    send_x,
    recv_x,
    send_y,
    recv_y,
    send_z,
    recv_z,
    send_s,
    recv_s,
    send_g,
    recv_g,
):
    n_z, n_x, n_y = grid_dims
    rows = ROWS // n_x
    me = lax.axis_index("space")
    dp = lax.axis_index("dp")
    zi = dp // (n_x * n_y)
    xi = lax.rem(dp // n_y, n_x)
    yi = lax.rem(dp, n_y)
    chip, core = me // 2, lax.rem(me, 2)
    near = jnp.where(chip == 1, 0, 1)
    far = 3 - chip - near
    space_peers = [
        2 * chip + 1 - core,
        2 * near + core,
        2 * near + 1 - core,
        2 * far + core,
        2 * far + 1 - core,
    ]
    second = jnp.where(chip == 0, 1 - core, jnp.where(chip == 2, core, 1))

    def band_of(turn):
        return jnp.where(turn == 0, 2, jnp.where(turn == 1, second, 1 - second))

    x_peers = [lax.rem(xi + r, n_x) for r in range(1, n_x)]
    y_peers = [lax.rem(yi + r, n_y) for r in range(1, n_y)]
    z_peers = [lax.rem(zi + r, n_z) for r in range(1, n_z)]

    def at_x(x):
        return {"dp": (zi * n_x + x) * n_y + yi}

    def at_y(y):
        return {"dp": (zi * n_x + xi) * n_y + y}

    def at_z(z):
        return {"dp": (z * n_x + xi) * n_y + yi}

    everyone = (
        [{"space": s} for s in space_peers]
        + [at_x(x) for x in x_peers]
        + [at_y(y) for y in y_peers]
        + [at_z(z) for z in z_peers]
    )
    barrier = pltpu.get_barrier_semaphore()
    for target in everyone:
        pl.semaphore_signal(barrier, inc=1, device_id=target, device_id_type=MESH)

    loads = [
        pltpu.make_async_copy(source, target, local_sem.at[index])
        for index, (source, target) in enumerate(
            (
                (plain_hbm, plain),
                (forward_hbm, forward_ref),
                (inverse_hbm, inverse_ref),
                (weight_hbm, weight_ref),
                (real_hbm, real_ref),
                (imag_hbm, imag_ref),
            )
        )
    ]
    for load in loads:
        load.start()
    mine_lanes = pl.ds(pl.multiple_of(me * SLICE, SLICE), SLICE)
    own_f = pltpu.make_async_copy(
        fields_ref.at[:, mine_lanes, :], field.at[pl.ds(me * BAND, BAND)], recv_f.at[me]
    )

    def offset(band, piece):
        start, size = PIECES[piece]
        return jnp.where(band < PARTS // 2, start, BAND - start - size)

    own_c = []
    for piece, (_, size) in enumerate(PIECES):
        start = offset(me, piece)
        own_c.append(
            pltpu.make_async_copy(
                cot_ref.at[pl.ds(start, size), mine_lanes, :],
                cot.at[pl.ds(me * BAND + start, size)],
                recv_c.at[me, piece],
            )
        )
    own_f.start()
    for copy in own_c:
        copy.start()
    pl.semaphore_wait(barrier, len(everyone))

    def exchange(source, target, send, recv):
        copies = []
        for slot, peer in enumerate(space_peers):
            lanes = pl.ds(pl.multiple_of(peer * SLICE, SLICE), SLICE)
            copies.append(
                pltpu.make_async_remote_copy(
                    src_ref=source.at[:, lanes, :],
                    dst_ref=target.at[pl.ds(me * BAND, BAND)],
                    send_sem=send.at[slot],
                    recv_sem=recv.at[me],
                    device_id={"space": peer},
                    device_id_type=MESH,
                )
            )
            copies[-1].start()
        return copies

    sends = exchange(fields_ref, field, send_f, recv_f)
    for slot, peer in enumerate(space_peers):
        lanes = pl.ds(pl.multiple_of(peer * SLICE, SLICE), SLICE)
        for piece, (_, size) in enumerate(PIECES):
            start = offset(me, piece)
            sends.append(
                pltpu.make_async_remote_copy(
                    src_ref=cot_ref.at[pl.ds(start, size), lanes, :],
                    dst_ref=cot.at[pl.ds(me * BAND + start, size)],
                    send_sem=send_c.at[slot, piece],
                    recv_sem=recv_c.at[me, piece],
                    device_id={"space": peer},
                    device_id_type=MESH,
                )
            )
            sends[-1].start()

    def arrive(target, recv, band):
        block = target.at[pl.ds(band * BAND, BAND)]
        pltpu.make_async_copy(block, block, recv.at[band]).wait()

    for load in loads:
        load.wait()

    lane = lax.broadcasted_iota(jnp.int32, (LANES, LANES), 1)
    degree = lax.broadcasted_iota(jnp.int32, (LANES, LANES), 0)
    even_row = lax.rem(degree, 2) == lane // ROWS
    for index, source in enumerate((real_ref, imag_ref)):
        acc[index] = jnp.zeros((LANES, LANES), jnp.float32)
        values = source[mine_lanes, :].astype(jnp.float32)
        acc[index, :, :MODES] = jnp.concatenate([values] * 4, axis=0)
        values = acc[index].T
        filt[0, index] = jnp.where(even_row, values, 0.0)
        filt[1, index] = jnp.where(even_row, 0.0, values)
    mixes[...] = jnp.zeros_like(mixes)
    work[pl.ds(HALF, LANES, stride=ROWS), :] = jnp.zeros((LANES, LANES), jnp.float32)
    @pl.loop(0, ORDERS // 4)
    def _(i):
        for index in range(4):
            turned[4 * i + index] = (
                plain[4 * i + index].astype(jnp.float32).T.astype(jnp.bfloat16)
            )

    zero = jnp.zeros((SLICE, NLON), jnp.bfloat16)

    def to_modes(pairs, basis_ref, first, factors):
        cosine = []
        sine = []
        for north, south in pairs:
            even = (north + south).astype(jnp.bfloat16)
            odd = (north - south).astype(jnp.bfloat16)
            cosine += [even, zero, odd, zero]
            sine += [zero, even, zero, odd]
        modes = dot(basis_ref[0], jnp.concatenate(cosine, axis=0), NT)
        modes += dot(basis_ref[1], jnp.concatenate(sine, axis=0), NT)
        for index in range(len(pairs)):
            part = modes[:, index * LANES : (index + 1) * LANES]
            if factors is not None:
                part = part * factors[index]
            work[pl.ds(first + index, LANES, stride=ROWS), :] = part

    @pl.loop(0, PARTS // 2)
    def _(turn):
        band = band_of(turn)
        arrive(field, recv_f, band)
        arrive(field, recv_f, PARTS - 1 - band)

        @pl.loop(0, BAND // STEP)
        def _(t):
            first = band * BAND + t * STEP
            js = [first + index for index in range(STEP)]
            to_modes(
                [
                    (
                        field[j].astype(jnp.float32),
                        field[NLAT - 1 - j].astype(jnp.float32),
                    )
                    for j in js
                ],
                forward_ref,
                first,
                [weight_ref[pl.ds(j, 1), :] for j in js],
            )

    odd_group = lax.rem(lane[:ROWS] // SLICE, 2) == 1

    def rows_of(m):
        return pl.ds(pl.multiple_of(m * ROWS, ROWS), ROWS)

    def synthesize(m, index):
        back_work[rows_of(m), :] = dot(plain[m], mixes[index])

    for low in range(0, ORDERS, 16):

        @pl.loop(0, 16 // UNROLL)
        def _(i, low=low):
            start = low + UNROLL * i
            for index in range(UNROLL):
                synthesize(jnp.maximum(start - UNROLL, 0) + index, index)
            for index in range(UNROLL):
                m = start + index
                modes = work[rows_of(m), :]
                turn = jnp.where(
                    odd_group,
                    pltpu.roll(modes, SLICE, 1),
                    -pltpu.roll(modes, LANES - SLICE, 1),
                )
                both = jnp.concatenate([modes, turn], axis=1).astype(jnp.bfloat16)
                full = dot(turned[m, low:, :], both)
                values, turn = full[:, :LANES], full[:, LANES:]
                parity = index % 2
                keep = even_row[low:] if parity == 0 else jnp.logical_not(even_row[low:])
                spec[m, low:, :] = jnp.where(keep, values, 0.0).astype(jnp.bfloat16)
                swap[m, low:, :] = jnp.where(keep, turn, 0.0).astype(jnp.bfloat16)
                mixed = values * filt[parity, 0, low:, :] + turn * filt[parity, 1, low:, :]
                mixed = mixed.astype(jnp.bfloat16)
                if low:
                    mixed = jnp.concatenate(
                        [jnp.zeros((low, LANES), jnp.bfloat16), mixed], axis=0
                    )
                mixes[index] = mixed

    for index in range(UNROLL):
        synthesize(ORDERS - UNROLL + index, index)

    @pl.loop(0, HALF // STEP)
    def _(t):
        for index in range(STEP):
            j = t * STEP + index
            modes = back_work[pl.ds(j, LANES, stride=ROWS), :].T
            north = (modes[:ROWS] + modes[ROWS:]).astype(jnp.bfloat16)
            south = (modes[:ROWS] - modes[ROWS:]).astype(jnp.bfloat16)
            cosine = jnp.concatenate([north[:SLICE], south[:SLICE]], axis=0)
            sine = jnp.concatenate([north[SLICE:], south[SLICE:]], axis=0)
            signal = dot(
                jnp.concatenate([cosine, sine], axis=1),
                inverse_ref[...].reshape(2 * LANES, NLON),
            )
            slope[j] = gelu_slope(signal)

    @pl.loop(0, PARTS // 2)
    def _(turn):
        band = band_of(turn)
        for piece, (begin, size) in enumerate(PIECES):
            for side in (band, PARTS - 1 - band):
                block = cot.at[pl.ds(side * BAND + offset(side, piece), size)]
                pltpu.make_async_copy(block, block, recv_c.at[side, piece]).wait()

            @pl.loop(0, size // STEP)
            def _(t, begin=begin):
                first = band * BAND + begin + t * STEP
                pairs = []
                for index in range(STEP):
                    j = first + index
                    north = cot[j].astype(jnp.float32) * slope[j, :SLICE]
                    south = cot[NLAT - 1 - j].astype(jnp.float32) * slope[j, SLICE:]
                    pairs.append((north, south))
                to_modes(pairs, inverse_ref, first, None)

    acc[...] = jnp.zeros_like(acc)
    for low in range(0, ORDERS, 16):
        spans = [
            (max(low, start), start + DEGREES)
            for start in range(0, ORDERS, DEGREES)
            if start + DEGREES > low
        ]

        @pl.loop(0, 16 // BACK_UNROLL)
        def _(i, low=low, spans=spans):
            for begin, end in spans:
                total = [acc[0, begin:end, :], acc[1, begin:end, :]]
                for index in range(BACK_UNROLL):
                    m = low + BACK_UNROLL * i + index
                    modes = work[rows_of(m), :].astype(jnp.bfloat16)
                    back = dot(turned[m, begin:end, :], modes)
                    total[0] += back * spec[m, begin:end, :].astype(jnp.float32)
                    total[1] += back * swap[m, begin:end, :].astype(jnp.float32)
                acc[0, begin:end, :] = total[0]
                acc[1, begin:end, :] = total[1]

    for index in range(2):
        total = acc[index].T * scale
        packed[pl.ds(index * SLICE, SLICE), :] = (
            total[:SLICE] + total[SLICE : 2 * SLICE]
        ) + (total[2 * SLICE : 3 * SLICE] + total[3 * SLICE :])

    def remote(src, dst, send, recv, target):
        copy = pltpu.make_async_remote_copy(
            src_ref=src,
            dst_ref=dst,
            send_sem=send,
            recv_sem=recv,
            device_id=target,
            device_id_type=MESH,
        )
        copy.start()
        return copy

    def piece(x):
        return pl.ds(pl.multiple_of(x * rows, rows), rows)

    copies = [
        remote(packed.at[piece(x)], xbuf.at[xi], send_x.at[r], recv_x.at[r], at_x(x))
        for r, x in enumerate(x_peers)
    ]
    xbuf[xi] = packed[piece(xi), :]
    for copy in copies:
        copy.wait()
    mine[0] = sum((xbuf[i] for i in range(1, n_x)), xbuf[0])

    copies = [
        remote(mine.at[0], ybuf.at[yi], send_y.at[r], recv_y.at[r], at_y(y))
        for r, y in enumerate(y_peers)
    ]
    ybuf[yi] = mine[0]
    for copy in copies:
        copy.wait()
    mine[1] = sum((ybuf[i] for i in range(1, n_y)), ybuf[0])

    copies = [
        remote(mine.at[1], zbuf.at[zi], send_z.at[r], recv_z.at[r], at_z(z))
        for r, z in enumerate(z_peers)
    ]
    zbuf[zi] = mine[1]
    for copy in copies:
        copy.wait()
    mine[2] = sum((zbuf[i] for i in range(1, n_z)), zbuf[0])

    spot = gathered.at[me, piece(xi)]
    copies = [
        remote(mine.at[2], spot, send_s.at[r], recv_s.at[me], {"space": s})
        for r, s in enumerate(space_peers)
    ]
    gathered[me, piece(xi)] = mine[2]
    for copy in copies:
        copy.wait_send()
    for s in space_peers:
        spot = gathered.at[s, piece(xi)]
        pltpu.make_async_copy(spot, spot, recv_s.at[s]).wait()

    column = gathered.at[:, piece(xi)]
    copies = [
        remote(column, column, send_g.at[r], recv_g.at[xi], at_x(x))
        for r, x in enumerate(x_peers)
    ]
    for copy in copies:
        copy.wait_send()
    for x in x_peers:
        spot = gathered.at[:, piece(x)]
        pltpu.make_async_copy(spot, spot, recv_g.at[x]).wait()

    for s in range(PARTS):
        for index in range(2):
            out_ref[index, s * SLICE : (s + 1) * SLICE, :] = gathered[
                s, index * SLICE : (index + 1) * SLICE, :MODES
            ]
    for copy in sends:
        copy.wait_send()


def on_device(grid_dims, batch, fields, cotangent, spec_real, spec_imag):
    n_z, n_x, n_y = grid_dims
    rows = ROWS // n_x
    weight, plain, forward, inverse = tables()
    fields = jnp.transpose(fields[0], (0, 2, 1))
    cotangent = jnp.transpose(cotangent[0], (0, 2, 1))
    vmem = pl.BlockSpec(memory_space=pltpu.VMEM)
    anywhere = pl.BlockSpec(memory_space=pl.ANY)
    out = jax.ShapeDtypeStruct((2, CHANNELS, MODES), jnp.float32)
    dma = pltpu.SemaphoreType.DMA
    result = pl.pallas_call(
        functools.partial(kernel, grid_dims, 1.0 / batch),
        out_shape=out,
        in_specs=[
            anywhere,
        ]
        * 8,
        out_specs=vmem,
        scratch_shapes=[
            pltpu.VMEM((NLAT, SLICE, NLON), jnp.bfloat16),
            pltpu.VMEM((NLAT, SLICE, NLON), jnp.bfloat16),
            pltpu.VMEM((ORDERS, ROWS, LANES), jnp.bfloat16),
            pltpu.VMEM((2, LANES, NLON), jnp.bfloat16),
            pltpu.VMEM((2, LANES, NLON), jnp.bfloat16),
            pltpu.VMEM((ROWS, LANES), jnp.float32),
            pltpu.VMEM((CHANNELS, MODES), jnp.bfloat16),
            pltpu.VMEM((CHANNELS, MODES), jnp.bfloat16),
            pltpu.VMEM((ORDERS, LANES, ROWS), jnp.bfloat16),
            pltpu.VMEM((ORDERS * ROWS, LANES), jnp.float32),
            pltpu.VMEM((ORDERS * ROWS, LANES), jnp.float32),
            pltpu.VMEM((HALF, ROWS, NLON), jnp.float32),
            pltpu.VMEM((ORDERS, LANES, LANES), jnp.bfloat16),
            pltpu.VMEM((ORDERS, LANES, LANES), jnp.bfloat16),
            pltpu.VMEM((2, 2, LANES, LANES), jnp.float32),
            pltpu.VMEM((UNROLL, LANES, LANES), jnp.bfloat16),
            pltpu.VMEM((2, LANES, LANES), jnp.float32),
            pltpu.VMEM((ROWS, LANES), jnp.float32),
            pltpu.VMEM((n_x, rows, LANES), jnp.float32),
            pltpu.VMEM((n_y, rows, LANES), jnp.float32),
            pltpu.VMEM((n_z, rows, LANES), jnp.float32),
            pltpu.VMEM((3, rows, LANES), jnp.float32),
            pltpu.VMEM((PARTS, ROWS, LANES), jnp.float32),
            dma((6,)),
            dma((PARTS,)),
            dma((PARTS,)),
            dma((PARTS, len(PIECES))),
            dma((PARTS, len(PIECES))),
            dma((n_x,)),
            dma((n_x,)),
            dma((n_y,)),
            dma((n_y,)),
            dma((n_z,)),
            dma((n_z,)),
            dma((PARTS,)),
            dma((PARTS,)),
            dma((n_x,)),
            dma((n_x,)),
        ],
        compiler_params=pltpu.CompilerParams(
            collective_id=0, has_side_effects=True, vmem_limit_bytes=56 * 2**20
        ),
    )(
        jnp.asarray(weight),
        fields,
        cotangent,
        jnp.asarray(plain),
        jnp.asarray(forward),
        jnp.asarray(inverse),
        spec_real.T,
        spec_imag.T,
    )
    return (result[0].T, result[1].T)


def solution(mesh):
    samples = mesh.shape["dp"]
    grid_dims = (4, 4, 8) if samples == 128 else (1, 1, 1)
    in_specs = (P("dp", "space", None, None), P("dp", "space", None, None), P(), P())
    return jax.shard_map(
        functools.partial(on_device, grid_dims, samples),
        mesh=mesh,
        in_specs=in_specs,
        out_specs=(P(), P()),
        check_vma=False,
    )
```

```python
import functools
import math

import jax
import jax.numpy as jnp
import ml_dtypes
import numpy as np
from jax import lax
from jax.experimental import pallas as pl
from jax.experimental.pallas import tpu as pltpu
from jax.sharding import PartitionSpec as P

NLAT = 126
NLON = 252
MODES = 126
ORDERS = 128
CHANNELS = 192
HALF = 63
PARTS = 6
BAND = 21
SLICE = 32
ROWS = 64
LANES = 128
STEP = 3
PIECES = ((0, 9), (9, 6), (15, 3), (18, 3))
UNROLL = 4
BACK_UNROLL = 16
DEGREES = 64
MESH = pl.DeviceIdType.MESH
NT = (((1,), (1,)), ((), ()))
NN = (((1,), (0,)), ((), ()))


def legendre_table(theta):
    counters = np.arange(1, MODES, dtype=np.float64)
    steps = 0.5 * np.log((2.0 * counters + 1.0) / (2.0 * counters))
    log_table = np.concatenate([np.zeros(1), np.cumsum(steps)])
    orders = np.arange(MODES, dtype=np.float64)[:, None]
    diagonal = np.exp(
        0.5 * np.log(1.0 / (4.0 * math.pi))
        + log_table[:, None]
        + orders * np.log(np.sin(theta))[None, :]
    )
    cosine = np.cos(theta)[None, :]
    previous = np.zeros_like(diagonal)
    earlier = np.zeros_like(diagonal)
    table = np.zeros((MODES, MODES, theta.size))
    for degree in range(MODES):
        growth = np.sqrt(
            max(4.0 * degree * degree - 1.0, 0.0)
            / np.maximum(degree * degree - orders * orders, 1.0)
        )
        below = degree - 1.0
        damping = np.sqrt(
            np.maximum(below * below - orders * orders, 0.0)
            / max(4.0 * below * below - 1.0, 1.0)
        )
        current = growth * (cosine * previous - damping * earlier)
        current = np.where(
            orders == degree, diagonal, np.where(orders < degree, current, 0.0)
        )
        table[:, degree] = current
        previous, earlier = current, previous
    return table


def tables():
    theta = math.pi * (np.arange(HALF) + 0.5) / NLAT
    weight = np.zeros((ROWS, LANES), np.float32)
    weight[:HALF] = (math.pi / NLAT * (2.0 * math.pi / NLON) * np.sin(theta))[:, None]
    plain = np.zeros((ORDERS, ROWS, LANES), np.float32)
    plain[:MODES, :HALF, :MODES] = legendre_table(theta).transpose(0, 2, 1)
    orders = np.arange(MODES)
    phase = orders[:, None] * np.arange(NLON)[None, :] % NLON
    angles = 2.0 * math.pi / NLON * phase
    basis = np.zeros((2, LANES, NLON), np.float32)
    basis[0, :MODES] = np.cos(angles)
    basis[1, :MODES] = -np.sin(angles)
    factor = np.full((LANES, 1), 2.0, np.float32)
    factor[0] = 1.0
    forward = basis.astype(ml_dtypes.bfloat16)
    inverse = (forward.astype(np.float32) * factor).astype(ml_dtypes.bfloat16)
    return weight, plain.astype(ml_dtypes.bfloat16), forward, inverse


def gelu_slope(values):
    cumulative = 0.5 * (1.0 + lax.erf(values * (1.0 / math.sqrt(2.0))))
    density = jnp.exp(-0.5 * values * values) * (1.0 / math.sqrt(2.0 * math.pi))
    return cumulative + values * density


def dot(a, b, dims=NN):
    return lax.dot_general(a, b, dims, preferred_element_type=jnp.float32)


def kernel(
    grid_dims,
    scale,
    weight_hbm,
    fields_ref,
    cot_ref,
    plain_hbm,
    forward_hbm,
    inverse_hbm,
    real_hbm,
    imag_hbm,
    out_ref,
    field,
    cot,
    plain,
    forward_ref,
    inverse_ref,
    weight_ref,
    real_ref,
    imag_ref,
    turned,
    work,
    back_work,
    slope,
    spec,
    swap,
    filt,
    mixes,
    acc,
    packed,
    xbuf,
    ybuf,
    zbuf,
    mine,
    final,
    gathered,
    local_sem,
    send_f,
    recv_f,
    send_c,
    recv_c,
    send_x,
    recv_x,
    send_y,
    recv_y,
    send_z,
    recv_z,
    send_s,
    recv_s,
    send_g,
    recv_g,
):
    n_z, n_x, n_y = grid_dims
    rows = ROWS // n_x
    me = lax.axis_index("space")
    dp = lax.axis_index("dp")
    zi = dp // (n_x * n_y)
    xi = lax.rem(dp // n_y, n_x)
    yi = lax.rem(dp, n_y)
    chip, core = me // 2, lax.rem(me, 2)
    near = jnp.where(chip == 1, 0, 1)
    far = 3 - chip - near
    space_peers = [
        2 * chip + 1 - core,
        2 * near + core,
        2 * near + 1 - core,
        2 * far + core,
        2 * far + 1 - core,
    ]
    second = jnp.where(chip == 0, 1 - core, jnp.where(chip == 2, core, 1))

    def band_of(turn):
        return jnp.where(turn == 0, 2, jnp.where(turn == 1, second, 1 - second))

    x_peers = [lax.rem(xi + r, n_x) for r in range(1, n_x)]
    y_peers = [lax.rem(yi + r, n_y) for r in range(1, n_y)]
    z_peers = [lax.rem(zi + r, n_z) for r in range(1, n_z)]

    def at_x(x):
        return {"dp": (zi * n_x + x) * n_y + yi}

    def at_y(y):
        return {"dp": (zi * n_x + xi) * n_y + y}

    def at_z(z):
        return {"dp": (z * n_x + xi) * n_y + yi}

    everyone = (
        [{"space": s} for s in space_peers]
        + [at_x(x) for x in x_peers]
        + [at_y(y) for y in y_peers]
        + [at_z(z) for z in z_peers]
    )
    barrier = pltpu.get_barrier_semaphore()
    for target in everyone:
        pl.semaphore_signal(barrier, inc=1, device_id=target, device_id_type=MESH)

    loads = [
        pltpu.make_async_copy(source, target, local_sem.at[index])
        for index, (source, target) in enumerate(
            (
                (plain_hbm, plain),
                (forward_hbm, forward_ref),
                (inverse_hbm, inverse_ref),
                (weight_hbm, weight_ref),
                (real_hbm, real_ref),
                (imag_hbm, imag_ref),
            )
        )
    ]
    for load in loads:
        load.start()
    mine_lanes = pl.ds(pl.multiple_of(me * SLICE, SLICE), SLICE)
    own_f = pltpu.make_async_copy(
        fields_ref.at[:, mine_lanes, :], field.at[pl.ds(me * BAND, BAND)], recv_f.at[me]
    )

    def offset(band, piece):
        start, size = PIECES[piece]
        return jnp.where(band < PARTS // 2, start, BAND - start - size)

    own_c = []
    for piece, (_, size) in enumerate(PIECES):
        start = offset(me, piece)
        own_c.append(
            pltpu.make_async_copy(
                cot_ref.at[pl.ds(start, size), mine_lanes, :],
                cot.at[pl.ds(me * BAND + start, size)],
                recv_c.at[me, piece],
            )
        )
    own_f.start()
    for copy in own_c:
        copy.start()
    pl.semaphore_wait(barrier, len(everyone))

    def exchange(source, target, send, recv):
        copies = []
        for slot, peer in enumerate(space_peers):
            lanes = pl.ds(pl.multiple_of(peer * SLICE, SLICE), SLICE)
            copies.append(
                pltpu.make_async_remote_copy(
                    src_ref=source.at[:, lanes, :],
                    dst_ref=target.at[pl.ds(me * BAND, BAND)],
                    send_sem=send.at[slot],
                    recv_sem=recv.at[me],
                    device_id={"space": peer},
                    device_id_type=MESH,
                )
            )
            copies[-1].start()
        return copies

    sends = exchange(fields_ref, field, send_f, recv_f)
    for slot, peer in enumerate(space_peers):
        lanes = pl.ds(pl.multiple_of(peer * SLICE, SLICE), SLICE)
        for piece, (_, size) in enumerate(PIECES):
            start = offset(me, piece)
            sends.append(
                pltpu.make_async_remote_copy(
                    src_ref=cot_ref.at[pl.ds(start, size), lanes, :],
                    dst_ref=cot.at[pl.ds(me * BAND + start, size)],
                    send_sem=send_c.at[slot, piece],
                    recv_sem=recv_c.at[me, piece],
                    device_id={"space": peer},
                    device_id_type=MESH,
                )
            )
            sends[-1].start()

    def arrive(target, recv, band):
        block = target.at[pl.ds(band * BAND, BAND)]
        pltpu.make_async_copy(block, block, recv.at[band]).wait()

    for load in loads:
        load.wait()

    lane = lax.broadcasted_iota(jnp.int32, (LANES, LANES), 1)
    degree = lax.broadcasted_iota(jnp.int32, (LANES, LANES), 0)
    even_row = lax.rem(degree, 2) == lane // ROWS
    for index, source in enumerate((real_ref, imag_ref)):
        acc[index] = jnp.zeros((LANES, LANES), jnp.float32)
        values = source[mine_lanes, :].astype(jnp.float32)
        acc[index, :, :MODES] = jnp.concatenate([values] * 4, axis=0)
        values = acc[index].T
        filt[0, index] = jnp.where(even_row, values, 0.0)
        filt[1, index] = jnp.where(even_row, 0.0, values)
    mixes[...] = jnp.zeros_like(mixes)
    work[pl.ds(HALF, LANES, stride=ROWS), :] = jnp.zeros((LANES, LANES), jnp.float32)
    @pl.loop(0, ORDERS // 4)
    def _(i):
        for index in range(4):
            turned[4 * i + index] = (
                plain[4 * i + index].astype(jnp.float32).T.astype(jnp.bfloat16)
            )

    zero = jnp.zeros((SLICE, NLON), jnp.bfloat16)

    def to_modes(pairs, basis_ref, first, factors):
        cosine = []
        sine = []
        for north, south in pairs:
            even = (north + south).astype(jnp.bfloat16)
            odd = (north - south).astype(jnp.bfloat16)
            cosine += [even, zero, odd, zero]
            sine += [zero, even, zero, odd]
        modes = dot(basis_ref[0], jnp.concatenate(cosine, axis=0), NT)
        modes += dot(basis_ref[1], jnp.concatenate(sine, axis=0), NT)
        for index in range(len(pairs)):
            part = modes[:, index * LANES : (index + 1) * LANES]
            if factors is not None:
                part = part * factors[index]
            work[pl.ds(first + index, LANES, stride=ROWS), :] = part

    @pl.loop(0, PARTS // 2)
    def _(turn):
        band = band_of(turn)
        arrive(field, recv_f, band)
        arrive(field, recv_f, PARTS - 1 - band)

        @pl.loop(0, BAND // STEP)
        def _(t):
            first = band * BAND + t * STEP
            js = [first + index for index in range(STEP)]
            to_modes(
                [
                    (
                        field[j].astype(jnp.float32),
                        field[NLAT - 1 - j].astype(jnp.float32),
                    )
                    for j in js
                ],
                forward_ref,
                first,
                [weight_ref[pl.ds(j, 1), :] for j in js],
            )

    odd_group = lax.rem(lane[:ROWS] // SLICE, 2) == 1

    def rows_of(m):
        return pl.ds(pl.multiple_of(m * ROWS, ROWS), ROWS)

    def synthesize(m, index):
        back_work[rows_of(m), :] = dot(plain[m], mixes[index])

    for low in range(0, ORDERS, 16):

        @pl.loop(0, 16 // UNROLL)
        def _(i, low=low):
            start = low + UNROLL * i
            for index in range(UNROLL):
                synthesize(jnp.maximum(start - UNROLL, 0) + index, index)
            for index in range(UNROLL):
                m = start + index
                modes = work[rows_of(m), :]
                turn = jnp.where(
                    odd_group,
                    pltpu.roll(modes, SLICE, 1),
                    -pltpu.roll(modes, LANES - SLICE, 1),
                )
                both = jnp.concatenate([modes, turn], axis=1).astype(jnp.bfloat16)
                full = dot(turned[m, low:, :], both)
                values, turn = full[:, :LANES], full[:, LANES:]
                parity = index % 2
                keep = even_row[low:] if parity == 0 else jnp.logical_not(even_row[low:])
                spec[m, low:, :] = jnp.where(keep, values, 0.0).astype(jnp.bfloat16)
                swap[m, low:, :] = jnp.where(keep, turn, 0.0).astype(jnp.bfloat16)
                mixed = values * filt[parity, 0, low:, :] + turn * filt[parity, 1, low:, :]
                mixed = mixed.astype(jnp.bfloat16)
                if low:
                    mixed = jnp.concatenate(
                        [jnp.zeros((low, LANES), jnp.bfloat16), mixed], axis=0
                    )
                mixes[index] = mixed

    for index in range(UNROLL):
        synthesize(ORDERS - UNROLL + index, index)

    @pl.loop(0, HALF // STEP)
    def _(t):
        for index in range(STEP):
            j = t * STEP + index
            modes = back_work[pl.ds(j, LANES, stride=ROWS), :].T
            north = (modes[:ROWS] + modes[ROWS:]).astype(jnp.bfloat16)
            south = (modes[:ROWS] - modes[ROWS:]).astype(jnp.bfloat16)
            cosine = jnp.concatenate([north[:SLICE], south[:SLICE]], axis=0)
            sine = jnp.concatenate([north[SLICE:], south[SLICE:]], axis=0)
            signal = dot(
                jnp.concatenate([cosine, sine], axis=1),
                inverse_ref[...].reshape(2 * LANES, NLON),
            )
            slope[j] = gelu_slope(signal)

    @pl.loop(0, PARTS // 2)
    def _(turn):
        band = band_of(turn)
        for piece, (begin, size) in enumerate(PIECES):
            for side in (band, PARTS - 1 - band):
                block = cot.at[pl.ds(side * BAND + offset(side, piece), size)]
                pltpu.make_async_copy(block, block, recv_c.at[side, piece]).wait()

            @pl.loop(0, size // STEP)
            def _(t, begin=begin):
                first = band * BAND + begin + t * STEP
                pairs = []
                for index in range(STEP):
                    j = first + index
                    north = cot[j].astype(jnp.float32) * slope[j, :SLICE]
                    south = cot[NLAT - 1 - j].astype(jnp.float32) * slope[j, SLICE:]
                    pairs.append((north, south))
                to_modes(pairs, inverse_ref, first, None)

    acc[...] = jnp.zeros_like(acc)
    for low in range(0, ORDERS, 16):
        spans = [
            (max(low, start), start + DEGREES)
            for start in range(0, ORDERS, DEGREES)
            if start + DEGREES > low
        ]

        @pl.loop(0, 16 // BACK_UNROLL)
        def _(i, low=low, spans=spans):
            for begin, end in spans:
                total = [acc[0, begin:end, :], acc[1, begin:end, :]]
                for index in range(BACK_UNROLL):
                    m = low + BACK_UNROLL * i + index
                    modes = work[rows_of(m), :].astype(jnp.bfloat16)
                    back = dot(turned[m, begin:end, :], modes)
                    total[0] += back * spec[m, begin:end, :].astype(jnp.float32)
                    total[1] += back * swap[m, begin:end, :].astype(jnp.float32)
                acc[0, begin:end, :] = total[0]
                acc[1, begin:end, :] = total[1]

    for index in range(2):
        total = acc[index].T * scale
        packed[pl.ds(index * SLICE, SLICE), :] = (
            total[:SLICE] + total[SLICE : 2 * SLICE]
        ) + (total[2 * SLICE : 3 * SLICE] + total[3 * SLICE :])

    def remote(src, dst, send, recv, target):
        copy = pltpu.make_async_remote_copy(
            src_ref=src,
            dst_ref=dst,
            send_sem=send,
            recv_sem=recv,
            device_id=target,
            device_id_type=MESH,
        )
        copy.start()
        return copy

    def piece(x):
        return pl.ds(pl.multiple_of(x * rows, rows), rows)

    copies = [
        remote(packed.at[piece(x)], xbuf.at[xi], send_x.at[r], recv_x.at[r], at_x(x))
        for r, x in enumerate(x_peers)
    ]
    xbuf[xi] = packed[piece(xi), :]
    for copy in copies:
        copy.wait()
    mine[0] = sum((xbuf[i] for i in range(1, n_x)), xbuf[0])

    copies = [
        remote(mine.at[0], ybuf.at[yi], send_y.at[r], recv_y.at[r], at_y(y))
        for r, y in enumerate(y_peers)
    ]
    ybuf[yi] = mine[0]
    for copy in copies:
        copy.wait()
    mine[1] = sum((ybuf[i] for i in range(1, n_y)), ybuf[0])

    copies = [
        remote(mine.at[1], zbuf.at[zi], send_z.at[r], recv_z.at[r], at_z(z))
        for r, z in enumerate(z_peers)
    ]
    zbuf[zi] = mine[1]
    for copy in copies:
        copy.wait()
    final[...] = sum((zbuf[i] for i in range(1, n_z)), zbuf[0]).astype(jnp.bfloat16)

    spot = gathered.at[me, piece(xi)]
    copies = [
        remote(final, spot, send_s.at[r], recv_s.at[me], {"space": s})
        for r, s in enumerate(space_peers)
    ]
    gathered[me, piece(xi)] = final[...]
    for copy in copies:
        copy.wait_send()
    for s in space_peers:
        spot = gathered.at[s, piece(xi)]
        pltpu.make_async_copy(spot, spot, recv_s.at[s]).wait()

    column = gathered.at[:, piece(xi)]
    copies = [
        remote(column, column, send_g.at[r], recv_g.at[xi], at_x(x))
        for r, x in enumerate(x_peers)
    ]
    for copy in copies:
        copy.wait_send()
    for x in x_peers:
        spot = gathered.at[:, piece(x)]
        pltpu.make_async_copy(spot, spot, recv_g.at[x]).wait()

    for s in range(PARTS):
        for index in range(2):
            out_ref[index, s * SLICE : (s + 1) * SLICE, :] = gathered[
                s, index * SLICE : (index + 1) * SLICE, :MODES
            ].astype(jnp.float32)
    for copy in sends:
        copy.wait_send()


def on_device(grid_dims, batch, fields, cotangent, spec_real, spec_imag):
    n_z, n_x, n_y = grid_dims
    rows = ROWS // n_x
    weight, plain, forward, inverse = tables()
    fields = jnp.transpose(fields[0], (0, 2, 1))
    cotangent = jnp.transpose(cotangent[0], (0, 2, 1))
    vmem = pl.BlockSpec(memory_space=pltpu.VMEM)
    anywhere = pl.BlockSpec(memory_space=pl.ANY)
    out = jax.ShapeDtypeStruct((2, CHANNELS, MODES), jnp.float32)
    dma = pltpu.SemaphoreType.DMA
    result = pl.pallas_call(
        functools.partial(kernel, grid_dims, 1.0 / batch),
        out_shape=out,
        in_specs=[
            anywhere,
        ]
        * 8,
        out_specs=vmem,
        scratch_shapes=[
            pltpu.VMEM((NLAT, SLICE, NLON), jnp.bfloat16),
            pltpu.VMEM((NLAT, SLICE, NLON), jnp.bfloat16),
            pltpu.VMEM((ORDERS, ROWS, LANES), jnp.bfloat16),
            pltpu.VMEM((2, LANES, NLON), jnp.bfloat16),
            pltpu.VMEM((2, LANES, NLON), jnp.bfloat16),
            pltpu.VMEM((ROWS, LANES), jnp.float32),
            pltpu.VMEM((CHANNELS, MODES), jnp.bfloat16),
            pltpu.VMEM((CHANNELS, MODES), jnp.bfloat16),
            pltpu.VMEM((ORDERS, LANES, ROWS), jnp.bfloat16),
            pltpu.VMEM((ORDERS * ROWS, LANES), jnp.float32),
            pltpu.VMEM((ORDERS * ROWS, LANES), jnp.float32),
            pltpu.VMEM((HALF, ROWS, NLON), jnp.float32),
            pltpu.VMEM((ORDERS, LANES, LANES), jnp.bfloat16),
            pltpu.VMEM((ORDERS, LANES, LANES), jnp.bfloat16),
            pltpu.VMEM((2, 2, LANES, LANES), jnp.float32),
            pltpu.VMEM((UNROLL, LANES, LANES), jnp.bfloat16),
            pltpu.VMEM((2, LANES, LANES), jnp.float32),
            pltpu.VMEM((ROWS, LANES), jnp.float32),
            pltpu.VMEM((n_x, rows, LANES), jnp.float32),
            pltpu.VMEM((n_y, rows, LANES), jnp.float32),
            pltpu.VMEM((n_z, rows, LANES), jnp.float32),
            pltpu.VMEM((2, rows, LANES), jnp.float32),
            pltpu.VMEM((rows, LANES), jnp.bfloat16),
            pltpu.VMEM((PARTS, ROWS, LANES), jnp.bfloat16),
            dma((6,)),
            dma((PARTS,)),
            dma((PARTS,)),
            dma((PARTS, len(PIECES))),
            dma((PARTS, len(PIECES))),
            dma((n_x,)),
            dma((n_x,)),
            dma((n_y,)),
            dma((n_y,)),
            dma((n_z,)),
            dma((n_z,)),
            dma((PARTS,)),
            dma((PARTS,)),
            dma((n_x,)),
            dma((n_x,)),
        ],
        compiler_params=pltpu.CompilerParams(
            collective_id=0, has_side_effects=True, vmem_limit_bytes=56 * 2**20
        ),
    )(
        jnp.asarray(weight),
        fields,
        cotangent,
        jnp.asarray(plain),
        jnp.asarray(forward),
        jnp.asarray(inverse),
        spec_real.T,
        spec_imag.T,
    )
    return (result[0].T, result[1].T)


def solution(mesh):
    samples = mesh.shape["dp"]
    grid_dims = (4, 4, 8) if samples == 128 else (1, 1, 1)
    in_specs = (P("dp", "space", None, None), P("dp", "space", None, None), P(), P())
    return jax.shard_map(
        functools.partial(on_device, grid_dims, samples),
        mesh=mesh,
        in_specs=in_specs,
        out_specs=(P(), P()),
        check_vma=False,
    )
```
